32 devices in a mesh: gx: 4 (over y, core), gy: 2 (over x), gz: 4 (over z).
Axes of the slice: x: 2, y: 2, z: 4, core: 2. Of those that a mesh axis runs over, the one named last changes fastest.
Arguments:
- positions: float32 [3, 4, 2, 4, 512], P(None, 'gx', 'gy', 'gz'), may hold values from 0 to 16, as said below
- charges: float32 [4, 2, 4, 512], P('gx', 'gy', 'gz'), may hold values from -4 to 4
- atom_types: int32 [4, 2, 4, 512], P('gx', 'gy', 'gz'), may hold values from 0 to 7
- type_table: float32 [3, 8], replicated, may hold values from 0.5 to 2
- live_count: int32 [4, 2, 4], P('gx', 'gy', 'gz'), may hold values from 358 to 512, as said below
- exp_map: float32 [64, 32, 64], P('gx', 'gy', 'gz'), may hold values from -6 to 6
Outputs:
- displacement: float32 [3, 4, 2, 4, 512], P(None, 'gx', 'gy', 'gz')
- last_force: float32 [3, 4, 2, 4, 512], P(None, 'gx', 'gy', 'gz')
- evolved: float32 [64, 32, 64], P('gx', 'gy', 'gz')
The draws below stay inside these ranges and needn't reach their ends.
Inputs may be any that keep to these rules, and one draw needn't show every extreme that they name: `positions`: each coordinate lies within its cell's brick: 0 to 16, 16, 16 along x, y, z. The live atoms of a cell are its first live_count slots; some cell has all 512 slots live.
All inputs are finite; a program needn't handle non-finite values.
Results may differ from the reference program's by a relative error of at most 0.0003.
Values sent between devices are 32-bit elements; how exact they have to be, the bound alone decides.
A program may use at most 128 MiB of HBM per device.

```python
import math
import jax
import jax.numpy as jnp
from jax import lax

BRICK_X = 16
BRICK_Y = 16
BRICK_Z = 16
ATOMS = 512
NTYPES = 8
SPLAT_MARGIN = 3
BLUR_REACH = 2
STEPS = 2
CELLS_X = 4
CELLS_Y = 2
CELLS_Z = 4
MAP_X = 64
MAP_Y = 32
MAP_Z = 64


def draw_positions(key, part):
    unit = jax.random.uniform(key, (3, CELLS_X, CELLS_Y, CELLS_Z, ATOMS), jnp.float32)
    extent = jnp.array([BRICK_X, BRICK_Y, BRICK_Z], jnp.float32).reshape(3, 1, 1, 1, 1)
    return (unit * extent).astype(jnp.float32)


def draw_live_count(key, part):
    key_one, key_two = jax.random.split(jax.random.fold_in(key, 17), 2)
    shape = (CELLS_X, CELLS_Y, CELLS_Z)
    counts = jax.random.randint(key_one, shape, 7 * ATOMS // 10, ATOMS + 1).reshape(-1)
    chosen = jax.random.randint(key_two, (), 0, CELLS_X * CELLS_Y * CELLS_Z)
    marker = jnp.arange(counts.shape[0], dtype=jnp.int32) == chosen
    return jnp.where(marker, ATOMS, counts).reshape(shape).astype(jnp.int32)


def place_ends(values, rng, smallest, top_value):
    shape = values.shape
    spot = [jax.random.randint(jax.random.fold_in(rng, axis), (), 0, shape[axis]) for axis in range(len(shape))]
    values = values.at[tuple(spot)].set(smallest)
    longest = shape.index(max(shape))
    spot[longest] = (spot[longest] + 1) % shape[longest]
    return values.at[tuple(spot)].set(top_value)


def steps_of(stream_key, dims, pieces, smallest, largest):
    def one(dim, blocks):
        draws = jax.random.uniform(jax.random.fold_in(jax.random.fold_in(stream_key, 6), dim), (blocks,), jnp.float32, smallest / len(pieces), largest / len(pieces))
        return jnp.repeat(jnp.exp(draws), dims[dim] // blocks).reshape((-1,) + (1,) * (len(dims) - dim - 1))

    level = one(*pieces[0])
    for cut in pieces[1:]:
        level = level * one(*cut)
    return level


def centred(rng, shape, deviation, most, pieces=(), kind=jnp.bfloat16):
    gain = steps_of(rng, shape, pieces, -0.22, 0.18) if pieces else 1.0
    values = jax.random.normal(rng, shape, jnp.float32) * deviation * gain
    return jnp.minimum(jnp.maximum(values, -most), most).astype(kind)


def setup_inputs(seed: int = 0) -> dict:
    seeds = jax.random.split(jax.random.key(seed), 7)
    return {
        "positions": draw_positions(jax.random.fold_in(seeds[6], 71), 0),
        "charges": centred(seeds[1], (CELLS_X, CELLS_Y, CELLS_Z, ATOMS), 1.0, 4.0, ((0, 4), (1, 2), (2, 4)), jnp.float32),
        "atom_types": place_ends(jax.random.randint(seeds[2], (CELLS_X, CELLS_Y, CELLS_Z, ATOMS), 0, NTYPES), jax.random.fold_in(seeds[2], 1), 0, NTYPES - 1).astype(jnp.int32),
        "type_table": jnp.clip(jnp.exp(jax.random.uniform(seeds[3], (3, NTYPES), jnp.float32, math.log(0.5), math.log(2.0))), 0.5, 2.0),
        "live_count": draw_live_count(jax.random.fold_in(seeds[6], 71), 0),
        "exp_map": centred(seeds[5], (MAP_X, MAP_Y, MAP_Z), 1.0, 6.0, ((0, 4), (1, 2), (2, 4)), jnp.float32),
    }


CUTOFF = 10.0
EPSILON = 1e-06
STEP_SIZE = 1.0
FIT_GAIN = 0.2

def pack_atoms(positions, charges, atom_types, type_table, live_count):
    type_total = type_table.shape[1]
    onehot = (atom_types[..., None] == jnp.arange(type_total, dtype=jnp.int32)).astype(jnp.float32)
    props = lax.optimization_barrier(jnp.sum(onehot[None] * type_table[:, None, None, None, None, :], axis=-1))
    slots = lax.broadcasted_iota(jnp.int32, charges.shape, 3)
    living = (slots < live_count[..., None]).astype(jnp.float32)
    return jnp.concatenate([positions, charges[None], props, living[None]], axis=0)

def block_list(nearby, brick_dims):
    channels = nearby.shape[0]
    slot_count = nearby.shape[-1]
    blocks = jnp.transpose(nearby.reshape(channels, 27, slot_count), (1, 0, 2))
    number = jnp.arange(27, dtype=jnp.int32)
    sides = jnp.stack([number // 9 - 1, number // 3 % 3 - 1, number % 3 - 1], axis=1).astype(jnp.float32)
    offsets = sides * jnp.array(brick_dims, jnp.float32)[None, :]
    centre = (number == 13).astype(jnp.float32)
    return (blocks, offsets, centre)

def geometry(own_atoms, block, offset):
    separation = own_atoms[0:3, :, None] - (block[0:3, None, :] + offset[:, None, None])
    squared = lax.optimization_barrier(jnp.sum(separation * separation, axis=0))
    smooth_cut = jnp.maximum(1.0 - squared / (CUTOFF * CUTOFF), 0.0)
    return (separation, squared, smooth_cut)

def born_radius(own_atoms, nearby, brick_dims):
    blocks, offsets, centre = block_list(nearby, brick_dims)
    slot_count = own_atoms.shape[1]
    identity_mask = jnp.eye(slot_count, dtype=jnp.float32)

    def visit(summed, element):
        block, offset, middle = element
        separation, squared, smooth_cut = geometry(own_atoms, block, offset)
        keep_mask = 1.0 - middle * identity_mask
        weight_term = jnp.exp(-squared / 8.0) * smooth_cut * smooth_cut * keep_mask * (block[5] * block[7])[None, :]
        return (summed + lax.optimization_barrier(jnp.sum(weight_term, axis=1)), None)
    summed, unused = lax.scan(visit, jnp.zeros((slot_count,), jnp.float32), (blocks, offsets, centre))
    return own_atoms[4] + summed

def gb_forces(own_atoms, own_radius, nearby, near_radius, brick_dims):
    blocks, offsets, centre = block_list(nearby, brick_dims)
    slot_count = own_atoms.shape[1]
    identity_mask = jnp.eye(slot_count, dtype=jnp.float32)
    radii = near_radius.reshape(27, slot_count)

    def visit(summed, element):
        block, radius_block, offset, middle = element
        separation, squared, smooth_cut = geometry(own_atoms, block, offset)
        product = own_radius[:, None] * radius_block[None, :]
        fading = jnp.exp(-squared / (4.0 * product))
        inverse = lax.rsqrt(squared + product * fading)
        charge_pair = (own_atoms[3] * own_atoms[7])[:, None] * (block[3] * block[7])[None, :] * (1.0 - middle * identity_mask)
        slope = -0.5 * charge_pair * (-2.0 * smooth_cut / (CUTOFF * CUTOFF) * inverse - 0.5 * smooth_cut * smooth_cut * inverse * inverse * inverse * (1.0 - 0.25 * fading))
        return (summed - 2.0 * lax.optimization_barrier(jnp.sum(slope[None] * separation, axis=2)), None)
    summed, unused = lax.scan(visit, jnp.zeros((3, slot_count), jnp.float32), (blocks, radii, offsets, centre))
    return summed

def profile(coord, start, stop, shift):
    points = jnp.arange(start, stop, dtype=jnp.float32)
    gap = points[None, :] - (coord[:, None] + shift)
    return (jnp.exp(-0.5 * gap * gap), gap)

def splat_extended(own_atoms, brick_dims):
    margin = SPLAT_MARGIN
    profile_x = profile(own_atoms[0], -margin, brick_dims[0] + margin, 0.0)[0]
    profile_y = profile(own_atoms[1], -margin, brick_dims[1] + margin, 0.0)[0]
    profile_z = profile(own_atoms[2], -margin, brick_dims[2] + margin, 0.0)[0]
    slot_count = own_atoms.shape[1]
    mass = own_atoms[6] * own_atoms[7]
    outer = (profile_y[:, :, None] * profile_z[:, None, :]).reshape(slot_count, -1)
    placed = jnp.dot((profile_x * mass[:, None]).T, outer, precision=lax.Precision.HIGHEST)
    return placed.reshape(profile_x.shape[1], profile_y.shape[1], profile_z.shape[1])

def kernel_weights(reach):
    values = [math.exp(-0.5 * (index - reach) ** 2) for index in range(2 * reach + 1)]
    whole = sum(values)
    return [value / whole for value in values]

def blur_axis(field, axis):
    weights = kernel_weights(BLUR_REACH)
    length = field.shape[axis]
    widths = [(0, 0), (0, 0), (0, 0)]
    widths[axis] = (BLUR_REACH, BLUR_REACH)
    padded = jnp.pad(field, widths)
    result = jnp.zeros_like(field)
    for index in range(len(weights)):
        result = result + weights[index] * lax.slice_in_dim(padded, index, index + length, axis=axis)
    return result

def blur_map(field):
    return blur_axis(blur_axis(blur_axis(field, 0), 1), 2)

def correlation_slope(evolved, exp_map, sums):
    squares, cross_sum, target = sums
    norm_value = jnp.sqrt((squares + EPSILON) * (target + EPSILON))
    score = cross_sum / norm_value
    return exp_map / norm_value - score * evolved / (squares + EPSILON)

def fit_force(grad_ext, own_atoms, brick_dims, scale):
    margin = SPLAT_MARGIN
    slot_count = own_atoms.shape[1]
    profile_x, gap_x = profile(own_atoms[0], -margin, brick_dims[0] + margin, 0.0)
    profile_y, gap_y = profile(own_atoms[1], -margin, brick_dims[1] + margin, 0.0)
    profile_z, gap_z = profile(own_atoms[2], -margin, brick_dims[2] + margin, 0.0)
    stacked = jnp.concatenate([profile_z, gap_z * profile_z], axis=0)
    inner = jnp.dot(grad_ext.reshape(-1, grad_ext.shape[2]), stacked.T, precision=lax.Precision.HIGHEST)
    inner = inner.reshape(grad_ext.shape[0], grad_ext.shape[1], 2 * slot_count)
    plain_z = inner[:, :, :slot_count]
    slope_z = inner[:, :, slot_count:]
    plain_y = jnp.einsum('ija,aj->ia', plain_z, profile_y, precision=lax.Precision.HIGHEST)
    turned_y = jnp.einsum('ija,aj->ia', plain_z, gap_y * profile_y, precision=lax.Precision.HIGHEST)
    turned_z = jnp.einsum('ija,aj->ia', slope_z, profile_y, precision=lax.Precision.HIGHEST)
    force = jnp.stack([lax.optimization_barrier(jnp.sum(gap_x * profile_x * plain_y.T, axis=1)), lax.optimization_barrier(jnp.sum(profile_x * turned_y.T, axis=1)), lax.optimization_barrier(jnp.sum(profile_x * turned_z.T, axis=1))])
    return scale * (own_atoms[6] * own_atoms[7])[None, :] * force

def per_cell(function, total):
    group = 16 if total % 16 == 0 else 1
    indices = jnp.arange(total, dtype=jnp.int32).reshape(-1, group)
    results = lax.map(jax.vmap(function), indices)
    return results.reshape((total,) + results.shape[2:])

def reference(positions, charges, atom_types, type_table, live_count, exp_map):
    brick_dims = (BRICK_X, BRICK_Y, BRICK_Z)
    packed = pack_atoms(positions, charges, atom_types, type_table, live_count)
    cell_total = CELLS_X * CELLS_Y * CELLS_Z
    cell_index = jnp.arange(cell_total, dtype=jnp.int32)
    scale = FIT_GAIN * float(MAP_X * MAP_Y * MAP_Z)
    anchor = jnp.zeros((), jnp.int32)
    current = positions
    force = jnp.zeros_like(positions)
    evolved = jnp.zeros_like(exp_map)

    def locate(index):
        cell_x = (index // (CELLS_Y * CELLS_Z)).astype(jnp.int32)
        cell_y = (index // CELLS_Z % CELLS_Y).astype(jnp.int32)
        cell_z = (index % CELLS_Z).astype(jnp.int32)
        return (cell_x, cell_y, cell_z)
    for step_index in range(STEPS):
        packed = jnp.concatenate([current, packed[3:]], axis=0)
        framed = jnp.pad(packed, ((0, 0), (1, 1), (1, 1), (1, 1), (0, 0)))

        def radius_cell(index):
            cell_x, cell_y, cell_z = locate(index)
            nearby = lax.dynamic_slice(framed, (anchor, cell_x, cell_y, cell_z, anchor), (8, 3, 3, 3, ATOMS))
            return born_radius(nearby[:, 1, 1, 1, :], nearby, brick_dims)
        radius = per_cell(radius_cell, cell_total).reshape(CELLS_X, CELLS_Y, CELLS_Z, ATOMS)
        radius_framed = jnp.pad(radius, ((1, 1), (1, 1), (1, 1), (0, 0)))

        def force_cell(index):
            cell_x, cell_y, cell_z = locate(index)
            nearby = lax.dynamic_slice(framed, (anchor, cell_x, cell_y, cell_z, anchor), (8, 3, 3, 3, ATOMS))
            near_radius = lax.dynamic_slice(radius_framed, (cell_x, cell_y, cell_z, anchor), (3, 3, 3, ATOMS))
            return gb_forces(nearby[:, 1, 1, 1, :], near_radius[1, 1, 1], nearby, near_radius, brick_dims)
        gb_part = per_cell(force_cell, cell_total)
        gb_part = jnp.transpose(gb_part, (1, 0, 2)).reshape(3, CELLS_X, CELLS_Y, CELLS_Z, ATOMS)

        def splat_cell(canvas, index):
            cell_x, cell_y, cell_z = locate(index)
            own_atoms = lax.dynamic_slice(packed, (anchor, cell_x, cell_y, cell_z, anchor), (8, 1, 1, 1, ATOMS))[:, 0, 0, 0, :]
            extended = splat_extended(own_atoms, brick_dims)
            start = (cell_x * BRICK_X, cell_y * BRICK_Y, cell_z * BRICK_Z)
            present = lax.dynamic_slice(canvas, start, extended.shape)
            return (lax.dynamic_update_slice(canvas, present + extended, start), None)
        canvas = jnp.zeros((MAP_X + 2 * SPLAT_MARGIN, MAP_Y + 2 * SPLAT_MARGIN, MAP_Z + 2 * SPLAT_MARGIN), jnp.float32)
        canvas, unused = lax.scan(splat_cell, canvas, cell_index)
        density = canvas[SPLAT_MARGIN:SPLAT_MARGIN + MAP_X, SPLAT_MARGIN:SPLAT_MARGIN + MAP_Y, SPLAT_MARGIN:SPLAT_MARGIN + MAP_Z]
        evolved = blur_map(density)
        sums = (jnp.sum(evolved * evolved), jnp.sum(evolved * exp_map), jnp.sum(exp_map * exp_map))
        sensitivity = correlation_slope(evolved, exp_map, sums)
        map_grad = blur_map(sensitivity)
        grad_framed = jnp.pad(map_grad, SPLAT_MARGIN)

        def fit_cell(index):
            cell_x, cell_y, cell_z = locate(index)
            own_atoms = lax.dynamic_slice(packed, (anchor, cell_x, cell_y, cell_z, anchor), (8, 1, 1, 1, ATOMS))[:, 0, 0, 0, :]
            grad_ext = lax.dynamic_slice(grad_framed, (cell_x * BRICK_X, cell_y * BRICK_Y, cell_z * BRICK_Z), (BRICK_X + 2 * SPLAT_MARGIN, BRICK_Y + 2 * SPLAT_MARGIN, BRICK_Z + 2 * SPLAT_MARGIN))
            return fit_force(grad_ext, own_atoms, brick_dims, scale)
        fit_part = per_cell(fit_cell, cell_total)
        fit_part = jnp.transpose(fit_part, (1, 0, 2)).reshape(3, CELLS_X, CELLS_Y, CELLS_Z, ATOMS)
        force = gb_part + fit_part
        current = current + STEP_SIZE * (packed[7][None] * force)
    return (current - positions, force, evolved)
```

```python
import functools
import math

import jax
import jax.numpy as jnp
from jax import lax
from jax.experimental import pallas as pl
from jax.experimental.pallas import tpu as pltpu
from jax.sharding import PartitionSpec as P

SPLAT_MARGIN = 3
BLUR_REACH = 2
STEPS = 2
CUTOFF = 10.0
EPSILON = 1e-06
STEP_SIZE = 1.0
FIT_GAIN = 0.2
REACH = SPLAT_MARGIN + BLUR_REACH
PAD = 8
LANES = 128
ROWS = 64
MESH = pl.DeviceIdType.MESH
AXES = ("gx", "gy", "gz")
VMEM = pl.BlockSpec(memory_space=pltpu.VMEM)
SMEM = pl.BlockSpec(memory_space=pltpu.SMEM)


def sides_of(number):
    return (number // 9 - 1, number // 3 % 3 - 1, number % 3 - 1)


def exchange_kernel(sizes, count, everyone, *refs):
    sources = refs[:count]
    position = count
    if everyone:
        part_ref = refs[position]
        position += 1
    outs = refs[position : position + count]
    position += count
    if everyone:
        parts_out = refs[position]
        position += 1
    send, recv = refs[position : position + 2]
    me = tuple(lax.axis_index(axis) for axis in AXES)
    total = sizes[0] * sizes[1] * sizes[2]
    mine = (me[0] * sizes[1] + me[1]) * sizes[2] + me[2]

    def exists(number):
        sides = sides_of(number)
        inside = None
        for axis in range(3):
            place = me[axis] + sides[axis]
            good = (place >= 0) & (place < sizes[axis])
            inside = good if inside is None else inside & good
        return inside

    def target(number):
        sides = sides_of(number)
        return tuple(me[axis] + sides[axis] for axis in range(3))

    def device_at(linear):
        return (
            linear // (sizes[1] * sizes[2]),
            linear // sizes[2] % sizes[1],
            linear % sizes[2],
        )

    others = [number for number in range(27) if number != 13]
    barrier = pltpu.get_barrier_semaphore()
    if everyone:

        def greet(step, carry):
            linear = lax.rem(mine + step, total)
            pl.semaphore_signal(barrier, inc=1, device_id=device_at(linear), device_id_type=MESH)
            return carry

        lax.fori_loop(1, total, greet, 0)
        pl.semaphore_wait(barrier, total - 1)
        send_all, recv_all = refs[position + 2 : position + 4]
    else:
        expected = 1
        for axis in range(3):
            low = jnp.where(me[axis] > 0, 1, 0)
            high = jnp.where(me[axis] < sizes[axis] - 1, 1, 0)
            expected = expected * (1 + low + high)
        for number in others:

            @pl.when(exists(number))
            def _(number=number):
                pl.semaphore_signal(barrier, inc=1, device_id=target(number), device_id_type=MESH)

        pl.semaphore_wait(barrier, expected - 1)

    def outgoing(index, number):
        return pltpu.make_async_remote_copy(
            src_ref=sources[index],
            dst_ref=outs[index].at[26 - number],
            send_sem=send.at[index, number],
            recv_sem=recv.at[index, 26 - number],
            device_id=target(number),
            device_id_type=MESH,
        )

    def arriving(index, number):
        return pltpu.make_async_remote_copy(
            src_ref=sources[index],
            dst_ref=outs[index].at[number],
            send_sem=send.at[index, number],
            recv_sem=recv.at[index, number],
            device_id=target(number),
            device_id_type=MESH,
        )

    def sum_copy(linear, slot):
        return pltpu.make_async_remote_copy(
            src_ref=part_ref,
            dst_ref=parts_out.at[slot],
            send_sem=send_all.at[linear],
            recv_sem=recv_all.at[slot],
            device_id=device_at(linear),
            device_id_type=MESH,
        )

    if everyone:

        def send_sum(step, carry):
            sum_copy(lax.rem(mine + step, total), mine).start()
            return carry

        lax.fori_loop(1, total, send_sum, 0)
    for number in others:

        @pl.when(exists(number))
        def _(number=number):
            for index in range(count):
                outgoing(index, number).start()

    for index in range(count):
        outs[index][13] = sources[index][...]
    if everyone:
        parts_out[mine] = part_ref[...]
    for number in others:

        @pl.when(jnp.logical_not(exists(number)))
        def _(number=number):
            for index in range(count):
                outs[index][number] = jnp.zeros(sources[index].shape, jnp.float32)

    for number in others:

        @pl.when(exists(number))
        def _(number=number):
            for index in range(count):
                outgoing(index, number).wait_send()
                arriving(index, number).wait_recv()

    if everyone:

        def wait_sum(step, carry):
            linear = lax.rem(mine + step, total)
            sum_copy(linear, mine).wait_send()
            sum_copy(linear, linear).wait_recv()
            return carry

        lax.fori_loop(1, total, wait_sum, 0)


def exchange(arrays, part, collective_id):
    sizes = tuple(lax.axis_size(axis) for axis in AXES)
    total = sizes[0] * sizes[1] * sizes[2]
    count = len(arrays)
    everyone = part is not None
    out_shape = [jax.ShapeDtypeStruct((27,) + a.shape, jnp.float32) for a in arrays]
    scratch = [pltpu.SemaphoreType.DMA((count, 27)), pltpu.SemaphoreType.DMA((count, 27))]
    operands = list(arrays)
    if everyone:
        operands.append(part)
        out_shape.append(jax.ShapeDtypeStruct((total,) + part.shape, jnp.float32))
        scratch += [pltpu.SemaphoreType.DMA((total,)), pltpu.SemaphoreType.DMA((total,))]
    return pl.pallas_call(
        functools.partial(exchange_kernel, sizes, count, everyone),
        out_shape=out_shape,
        in_specs=[VMEM] * len(operands),
        out_specs=[VMEM] * len(out_shape),
        scratch_shapes=scratch,
        compiler_params=pltpu.CompilerParams(collective_id=collective_id, has_side_effects=True),
        name=f"exchange{collective_id}",
    )(*operands)


def kernel_weights(reach):
    values = [math.exp(-0.5 * (index - reach) ** 2) for index in range(2 * reach + 1)]
    whole = sum(values)
    return [value / whole for value in values]


def spread(values):
    weights = kernel_weights(BLUR_REACH)
    rows = values.shape[0]
    result = weights[BLUR_REACH] * values
    for shift in range(1, BLUR_REACH + 1):
        both = pltpu.roll(values, shift, 0) + pltpu.roll(values, rows - shift, 0)
        result = result + weights[BLUR_REACH + shift] * both
    return result


def profile_rows(coord, side, length, place, extent, slope):
    rows = length + 2 * PAD
    point = lax.broadcasted_iota(jnp.int32, (rows, coord.shape[-1]), 0) - PAD
    within = point + place * length
    start = side * length
    grid = (within >= 0) & (within < extent * length)
    window = grid & (point >= start - SPLAT_MARGIN) & (point < start + length + SPLAT_MARGIN)
    reach = grid & (point >= start - REACH) & (point < start + length + REACH)
    offset = jnp.asarray(side * length, jnp.float32)
    gap = point.astype(jnp.float32) - (coord + offset)
    plain = jnp.where(window, jnp.exp(-0.5 * gap * gap), 0.0)
    wide = jnp.where(reach, spread(plain), 0.0)
    if not slope:
        return wide
    return wide, jnp.where(reach, spread(gap * plain), 0.0)


def born_kernel(dims, near_ref, own_ref, list_ref, count_ref, out_ref):
    slots = near_ref.shape[-1]
    pieces = slots // LANES

    def block(index, carry):
        base = pl.multiple_of(index * ROWS, ROWS)
        own = [
            jnp.broadcast_to(own_ref[pl.ds(base, ROWS), k : k + 1], (ROWS, LANES))
            for k in range(3)
        ]

        def visit(step, summed):
            number = list_ref[index, step]
            cell = number // pieces
            lane = pl.multiple_of(number % pieces * LANES, LANES)
            sides = sides_of(cell)
            squared = None
            for axis in range(3):
                row = near_ref[cell, axis : axis + 1, pl.ds(lane, LANES)]
                shift = sides[axis].astype(jnp.float32) * float(dims[axis])
                gap = own[axis] - (row + shift)
                squared = gap * gap if squared is None else squared + gap * gap
            smooth = jnp.maximum(1.0 - squared * (1.0 / (CUTOFF * CUTOFF)), 0.0)
            weight = near_ref[cell, 4:5, pl.ds(lane, LANES)]
            return summed + jnp.exp(squared * -0.125) * (smooth * smooth) * weight

        summed = lax.fori_loop(
            0, count_ref[0, index], visit, jnp.zeros((ROWS, LANES), jnp.float32)
        )
        own_screen = own_ref[pl.ds(base, ROWS), 4:5]
        radius = own_ref[pl.ds(base, ROWS), 6:7]
        out_ref[pl.ds(base, ROWS), :] = radius + (
            jnp.sum(summed, axis=1, keepdims=True) - own_screen
        )
        return carry

    lax.fori_loop(0, slots // ROWS, block, 0)


def force_kernel(dims, near_ref, radii_ref, own_ref, radius_ref, list_ref, count_ref, out_ref):
    slots = near_ref.shape[-1]
    pieces = slots // LANES

    def block(index, carry):
        base = pl.multiple_of(index * ROWS, ROWS)
        own = [
            jnp.broadcast_to(own_ref[pl.ds(base, ROWS), k : k + 1], (ROWS, LANES))
            for k in range(3)
        ]
        radius = jnp.broadcast_to(radius_ref[pl.ds(base, ROWS), :], (ROWS, LANES))
        inverse_radius = -0.25 / radius

        def visit(step, summed):
            number = list_ref[index, step]
            cell = number // pieces
            lane = pl.multiple_of(number % pieces * LANES, LANES)
            sides = sides_of(cell)
            squared = None
            gaps = []
            for axis in range(3):
                row = near_ref[cell, axis : axis + 1, pl.ds(lane, LANES)]
                shift = sides[axis].astype(jnp.float32) * float(dims[axis])
                gap = own[axis] - (row + shift)
                gaps.append(gap)
                squared = gap * gap if squared is None else squared + gap * gap
            smooth = jnp.maximum(1.0 - squared * (1.0 / (CUTOFF * CUTOFF)), 0.0)
            near_radius = radii_ref[cell, :, pl.ds(lane, LANES)]
            charge = near_ref[cell, 3:4, pl.ds(lane, LANES)]
            fading = jnp.exp(squared * (inverse_radius * (1.0 / near_radius)))
            inverse = lax.rsqrt(squared + (radius * near_radius) * fading)
            common = (
                (charge * (smooth * inverse))
                * (
                    2.0 / (CUTOFF * CUTOFF)
                    + (smooth * (inverse * inverse)) * (0.5 - 0.125 * fading)
                )
            )
            return tuple(total + common * gap for total, gap in zip(summed, gaps))

        zero = jnp.zeros((ROWS, LANES), jnp.float32)
        summed = lax.fori_loop(0, count_ref[0, index], visit, (zero, zero, zero))
        charge = own_ref[pl.ds(base, ROWS), 3:4]
        for axis in range(3):
            out_ref[pl.ds(base, ROWS), axis : axis + 1] = -charge * jnp.sum(
                summed[axis], axis=1, keepdims=True
            )
        return carry

    lax.fori_loop(0, slots // ROWS, block, 0)


def halves(value):
    high = value.astype(jnp.bfloat16)
    return high, (value - high.astype(jnp.float32)).astype(jnp.bfloat16)


def evolved_kernel(dims, sizes, near_ref, place_ref, out_ref, px_ref, py_ref, pz_ref, total_ref):
    places = [place_ref[0, k] for k in range(3)]
    depth = dims[2] + 2 * PAD

    def profiles(cell, carry):
        sides = sides_of(cell)
        made = [
            profile_rows(
                near_ref[cell, axis : axis + 1, :],
                sides[axis],
                dims[axis],
                places[axis],
                sizes[axis],
                False,
            )
            for axis in range(3)
        ]
        px_ref[cell] = made[0] * near_ref[cell, 5:6, :]
        py_ref[cell] = made[1]
        high, low = halves(made[2])
        pz_ref[cell, 0:depth, :] = high
        pz_ref[cell, depth : 2 * depth, :] = low
        return carry

    lax.fori_loop(0, 27, profiles, 0)
    half_x = dims[0] // 2 + REACH
    half_y = dims[1] // 2 + PAD
    rows = half_x * half_y
    for hx in range(2):
        first = PAD - REACH if hx == 0 else PAD + dims[0] // 2
        for hy in range(2):
            total_ref[...] = jnp.zeros_like(total_ref)

            def add(step, carry):
                cell = (hx + step // 6) * 9 + (hy + step // 3 % 2) * 3 + step % 3
                py = py_ref[cell, hy * half_y : (hy + 1) * half_y, :]
                pieces_high, pieces_low = [], []
                for k in range(half_x):
                    high, low = halves(px_ref[cell, first + k : first + k + 1, :] * py)
                    pieces_high.append(high)
                    pieces_low.append(low)
                plane = jnp.concatenate(pieces_high + pieces_low, axis=0)
                total_ref[...] += lax.dot_general(
                    plane,
                    pz_ref[cell],
                    (((1,), (1,)), ((), ())),
                    preferred_element_type=jnp.float32,
                )
                return carry

            lax.fori_loop(0, 12, add, 0)
            result = (
                total_ref[0:rows, 0:depth]
                + total_ref[0:rows, depth : 2 * depth]
                + total_ref[rows : 2 * rows, 0:depth]
            )
            out_ref[
                hx * half_x : (hx + 1) * half_x, hy * half_y : (hy + 1) * half_y, :
            ] = result.reshape(half_x, half_y, depth)


def fit_kernel(dims, sizes, own_ref, place_ref, sens_ref, out_ref, big_ref):
    places = [place_ref[0, k] for k in range(3)]
    slots = own_ref.shape[-1]
    wide = []
    slope = []
    for axis in range(3):
        a, b = profile_rows(
            own_ref[axis : axis + 1, :], 0, dims[axis], places[axis], sizes[axis], True
        )
        wide.append(a)
        slope.append(b)
    both = jnp.concatenate([wide[2], slope[2]], axis=1)
    high, low = halves(both)
    right = jnp.concatenate([high, low, high], axis=0)
    big_ref[...] = jnp.dot(sens_ref[...], right, preferred_element_type=jnp.float32)
    height = dims[1] + 2 * PAD
    force = [jnp.zeros((1, slots), jnp.float32) for _ in range(3)]
    for k in range(dims[0] + 2 * REACH):
        row = PAD - REACH + k
        plain_z = big_ref[k * height : (k + 1) * height, 0:slots]
        slope_z = big_ref[k * height : (k + 1) * height, slots : 2 * slots]
        plain = jnp.sum(plain_z * wide[1], axis=0, keepdims=True)
        turned_y = jnp.sum(plain_z * slope[1], axis=0, keepdims=True)
        turned_z = jnp.sum(slope_z * wide[1], axis=0, keepdims=True)
        here = wide[0][row : row + 1, :]
        force[0] = force[0] + slope[0][row : row + 1, :] * plain
        force[1] = force[1] + here * turned_y
        force[2] = force[2] + here * turned_z
    mass = own_ref[5:6, :]
    for axis in range(3):
        out_ref[axis : axis + 1, :] = mass * force[axis]


def frame_map(bricks, dims):
    reaches = (REACH, PAD, PAD)
    cube = bricks.reshape((3, 3, 3) + dims)

    def join(parts, axis):
        length = dims[axis]
        return jnp.concatenate(
            [
                lax.slice_in_dim(parts[0], length - reaches[axis], length, axis=axis),
                parts[1],
                lax.slice_in_dim(parts[2], 0, reaches[axis], axis=axis),
            ],
            axis=axis,
        )

    return join(
        [join([join([cube[a, b, c] for c in range(3)], 2) for b in range(3)], 1) for a in range(3)],
        0,
    )


def active_lists(near, dims):
    slots = near.shape[-1]
    pieces = slots // LANES
    blocks = slots // ROWS
    number = jnp.arange(27, dtype=jnp.int32)
    sides = jnp.stack(sides_of(number), axis=1).astype(jnp.float32)
    offsets = sides * jnp.array(dims, jnp.float32)[None, :]
    coords = near[:, 0:3, :] + offsets[:, :, None]
    live = near[:, 7:8, :] > 0.5
    big = 1e30
    low = jnp.where(live, coords, big).reshape(27, 3, pieces, LANES).min(axis=-1)
    high = jnp.where(live, coords, -big).reshape(27, 3, pieces, LANES).max(axis=-1)
    own_low = jnp.where(live[13], coords[13], big).reshape(3, blocks, ROWS).min(axis=-1)
    own_high = jnp.where(live[13], coords[13], -big).reshape(3, blocks, ROWS).max(axis=-1)
    apart = jnp.maximum(
        low[:, :, :, None] - own_high[None, :, None, :],
        own_low[None, :, None, :] - high[:, :, :, None],
    )
    apart = jnp.maximum(apart, 0.0)
    keep = jnp.sum(apart * apart, axis=1) < CUTOFF * CUTOFF * 1.001
    keep = keep.reshape(27 * pieces, blocks).T
    whole = 27 * pieces
    index = jnp.arange(whole, dtype=jnp.int32)
    before = (index[:, None] <= index[None, :]).astype(jnp.bfloat16)
    spot = jnp.dot(
        keep.astype(jnp.bfloat16), before, preferred_element_type=jnp.float32
    ).astype(jnp.int32)
    counts = spot[:, -1]
    chosen = keep[:, :, None] & (spot[:, :, None] - 1 == index[None, None, :])
    lists = jnp.sum(jnp.where(chosen, index[None, :, None], 0), axis=1)
    return lists, counts[None, :]


def on_device(positions, charges, atom_types, type_table, live_count, exp_map):
    dims = exp_map.shape
    sizes = tuple(lax.axis_size(axis) for axis in AXES)
    slots = positions.shape[-1]
    grid_points = dims[0] * dims[1] * dims[2] * sizes[0] * sizes[1] * sizes[2]
    scale = FIT_GAIN * float(grid_points)
    place = jnp.stack([lax.axis_index(axis) for axis in AXES]).astype(jnp.int32).reshape(1, 3)

    kinds = jnp.arange(type_table.shape[1], dtype=jnp.int32)
    onehot = (atom_types.reshape(1, slots) == kinds[:, None]).astype(jnp.float32)
    props = jnp.sum(type_table[:, :, None] * onehot[None], axis=1)
    living = (
        lax.broadcasted_iota(jnp.int32, (1, slots), 1) < live_count.reshape(1, 1)
    ).astype(jnp.float32)
    start = positions.reshape(3, slots)
    fixed = jnp.concatenate(
        [
            charges.reshape(1, slots) * living,
            props[1:2] * living,
            props[2:3] * living,
            props[0:1],
            living,
        ],
        axis=0,
    )
    current = start
    target = jnp.sum(exp_map * exp_map)
    framed = None
    for step in range(STEPS):
        own = jnp.concatenate([current, fixed], axis=0)
        if step == 0:
            near, bricks = exchange([own, exp_map.reshape(-1, LANES)], None, 0)
            framed = frame_map(bricks, dims)
        else:
            (near,) = exchange([own], None, 1)
        columns = own.T
        lists, counts = active_lists(near, dims)
        radius = pl.pallas_call(
            functools.partial(born_kernel, dims),
            out_shape=jax.ShapeDtypeStruct((slots, 1), jnp.float32),
            in_specs=[VMEM, VMEM, SMEM, SMEM],
            out_specs=VMEM,
            name="born",
        )(near, columns, lists, counts)
        wide = pl.pallas_call(
            functools.partial(evolved_kernel, dims, sizes),
            out_shape=jax.ShapeDtypeStruct(
                (dims[0] + 2 * REACH, dims[1] + 2 * PAD, dims[2] + 2 * PAD), jnp.float32
            ),
            in_specs=[VMEM, SMEM],
            out_specs=VMEM,
            scratch_shapes=[
                pltpu.VMEM((27, dims[0] + 2 * PAD, slots), jnp.float32),
                pltpu.VMEM((27, dims[1] + 2 * PAD, slots), jnp.float32),
                pltpu.VMEM((27, 2 * (dims[2] + 2 * PAD), slots), jnp.bfloat16),
                pltpu.VMEM(
                    (
                        2 * (dims[0] // 2 + REACH) * (dims[1] // 2 + PAD),
                        2 * (dims[2] + 2 * PAD),
                    ),
                    jnp.float32,
                ),
            ],
            name="evolve",
        )(near, place)
        evolved = wide[
            REACH : REACH + dims[0], PAD : PAD + dims[1], PAD : PAD + dims[2]
        ]
        lane = lax.broadcasted_iota(jnp.int32, (1, LANES), 1)
        part = jnp.where(
            lane == 0,
            jnp.sum(evolved * evolved),
            jnp.where(lane == 1, jnp.sum(evolved * exp_map), jnp.where(lane == 2, target, 0.0)),
        )
        near_radius, parts = exchange([radius.reshape(1, slots)], part, 2)
        sums = jnp.sum(parts, axis=(0, 1))
        squares, cross_sum, whole_target = sums[0], sums[1], sums[2]
        norm = jnp.sqrt((squares + EPSILON) * (whole_target + EPSILON))
        score = cross_sum / norm
        sensitivity = framed / norm - score * wide / (squares + EPSILON)
        sensitivity = sensitivity.reshape(-1, sensitivity.shape[-1])
        rounded = lax.reduce_precision(sensitivity, 8, 7)
        high, low = rounded.astype(jnp.bfloat16), (sensitivity - rounded).astype(jnp.bfloat16)
        stacked = jnp.concatenate([high, high, low], axis=1)
        fit = pl.pallas_call(
            functools.partial(fit_kernel, dims, sizes),
            out_shape=jax.ShapeDtypeStruct((3, slots), jnp.float32),
            in_specs=[VMEM, SMEM, VMEM],
            out_specs=VMEM,
            scratch_shapes=[pltpu.VMEM((stacked.shape[0], 2 * slots), jnp.float32)],
            name="fit",
        )(own, place, stacked)
        pair = pl.pallas_call(
            functools.partial(force_kernel, dims),
            out_shape=jax.ShapeDtypeStruct((slots, 3), jnp.float32),
            in_specs=[VMEM, VMEM, VMEM, VMEM, SMEM, SMEM],
            out_specs=VMEM,
            name="pair",
        )(near, near_radius, columns, radius, lists, counts)
        force = pair.T + scale * fit
        current = current + STEP_SIZE * (living * force)
    shape = positions.shape
    return ((current - start).reshape(shape), force.reshape(shape), evolved)


def solution(mesh):
    placed = (
        P(None, "gx", "gy", "gz", None),
        P("gx", "gy", "gz", None),
        P("gx", "gy", "gz", None),
        P(),
        P("gx", "gy", "gz"),
        P("gx", "gy", "gz"),
    )
    return jax.shard_map(
        on_device,
        mesh=mesh,
        in_specs=placed,
        out_specs=(
            P(None, "gx", "gy", "gz", None),
            P(None, "gx", "gy", "gz", None),
            P("gx", "gy", "gz"),
        ),
        check_vma=False,
    )
```

```python
import functools
import math

import jax
import jax.numpy as jnp
from jax import lax
from jax.experimental import pallas as pl
from jax.experimental.pallas import tpu as pltpu
from jax.sharding import PartitionSpec as P

SPLAT_MARGIN = 3
BLUR_REACH = 2
STEPS = 2
CUTOFF = 10.0
EPSILON = 1e-06
STEP_SIZE = 1.0
FIT_GAIN = 0.2
REACH = SPLAT_MARGIN + BLUR_REACH
PAD = 8
LANES = 128
ROWS = 64
MESH = pl.DeviceIdType.MESH
AXES = ("gx", "gy", "gz")
VMEM = pl.BlockSpec(memory_space=pltpu.VMEM)
SMEM = pl.BlockSpec(memory_space=pltpu.SMEM)


def sides_of(number):
    return (number // 9 - 1, number // 3 % 3 - 1, number % 3 - 1)


def exchange_kernel(sizes, count, everyone, *refs):
    sources = refs[:count]
    position = count
    if everyone:
        part_ref = refs[position]
        position += 1
    outs = refs[position : position + count]
    position += count
    if everyone:
        parts_out = refs[position]
        position += 1
    send, recv = refs[position : position + 2]
    me = tuple(lax.axis_index(axis) for axis in AXES)
    total = sizes[0] * sizes[1] * sizes[2]
    mine = (me[0] * sizes[1] + me[1]) * sizes[2] + me[2]

    def exists(number):
        sides = sides_of(number)
        inside = None
        for axis in range(3):
            place = me[axis] + sides[axis]
            good = (place >= 0) & (place < sizes[axis])
            inside = good if inside is None else inside & good
        return inside

    def target(number):
        sides = sides_of(number)
        return tuple(me[axis] + sides[axis] for axis in range(3))

    def device_at(linear):
        return (
            linear // (sizes[1] * sizes[2]),
            linear // sizes[2] % sizes[1],
            linear % sizes[2],
        )

    others = [number for number in range(27) if number != 13]
    barrier = pltpu.get_barrier_semaphore()
    if everyone:

        def greet(step, carry):
            linear = lax.rem(mine + step, total)
            pl.semaphore_signal(barrier, inc=1, device_id=device_at(linear), device_id_type=MESH)
            return carry

        lax.fori_loop(1, total, greet, 0)
        pl.semaphore_wait(barrier, total - 1)
        send_all, recv_all = refs[position + 2 : position + 4]
    else:
        expected = 1
        for axis in range(3):
            low = jnp.where(me[axis] > 0, 1, 0)
            high = jnp.where(me[axis] < sizes[axis] - 1, 1, 0)
            expected = expected * (1 + low + high)
        for number in others:

            @pl.when(exists(number))
            def _(number=number):
                pl.semaphore_signal(barrier, inc=1, device_id=target(number), device_id_type=MESH)

        pl.semaphore_wait(barrier, expected - 1)

    def outgoing(index, number):
        return pltpu.make_async_remote_copy(
            src_ref=sources[index],
            dst_ref=outs[index].at[26 - number],
            send_sem=send.at[index, number],
            recv_sem=recv.at[index, 26 - number],
            device_id=target(number),
            device_id_type=MESH,
        )

    def arriving(index, number):
        return pltpu.make_async_remote_copy(
            src_ref=sources[index],
            dst_ref=outs[index].at[number],
            send_sem=send.at[index, number],
            recv_sem=recv.at[index, number],
            device_id=target(number),
            device_id_type=MESH,
        )

    def sum_copy(linear, slot):
        return pltpu.make_async_remote_copy(
            src_ref=part_ref,
            dst_ref=parts_out.at[slot],
            send_sem=send_all.at[linear],
            recv_sem=recv_all.at[slot],
            device_id=device_at(linear),
            device_id_type=MESH,
        )

    if everyone:

        def send_sum(step, carry):
            sum_copy(lax.rem(mine + step, total), mine).start()
            return carry

        lax.fori_loop(1, total, send_sum, 0)
    for number in others:

        @pl.when(exists(number))
        def _(number=number):
            for index in range(count):
                outgoing(index, number).start()

    for index in range(count):
        outs[index][13] = sources[index][...]
    if everyone:
        parts_out[mine] = part_ref[...]
    for number in others:

        @pl.when(jnp.logical_not(exists(number)))
        def _(number=number):
            for index in range(count):
                outs[index][number] = jnp.zeros(sources[index].shape, jnp.float32)

    for number in others:

        @pl.when(exists(number))
        def _(number=number):
            for index in range(count):
                outgoing(index, number).wait_send()
                arriving(index, number).wait_recv()

    if everyone:

        def wait_sum(step, carry):
            linear = lax.rem(mine + step, total)
            sum_copy(linear, mine).wait_send()
            sum_copy(linear, linear).wait_recv()
            return carry

        lax.fori_loop(1, total, wait_sum, 0)


def exchange(arrays, part, collective_id):
    sizes = tuple(lax.axis_size(axis) for axis in AXES)
    total = sizes[0] * sizes[1] * sizes[2]
    count = len(arrays)
    everyone = part is not None
    out_shape = [jax.ShapeDtypeStruct((27,) + a.shape, jnp.float32) for a in arrays]
    scratch = [pltpu.SemaphoreType.DMA((count, 27)), pltpu.SemaphoreType.DMA((count, 27))]
    operands = list(arrays)
    if everyone:
        operands.append(part)
        out_shape.append(jax.ShapeDtypeStruct((total,) + part.shape, jnp.float32))
        scratch += [pltpu.SemaphoreType.DMA((total,)), pltpu.SemaphoreType.DMA((total,))]
    return pl.pallas_call(
        functools.partial(exchange_kernel, sizes, count, everyone),
        out_shape=out_shape,
        in_specs=[VMEM] * len(operands),
        out_specs=[VMEM] * len(out_shape),
        scratch_shapes=scratch,
        compiler_params=pltpu.CompilerParams(collective_id=collective_id, has_side_effects=True),
        name=f"exchange{collective_id}",
    )(*operands)


def kernel_weights(reach):
    values = [math.exp(-0.5 * (index - reach) ** 2) for index in range(2 * reach + 1)]
    whole = sum(values)
    return [value / whole for value in values]


def spread(values):
    weights = kernel_weights(BLUR_REACH)
    rows = values.shape[0]
    result = weights[BLUR_REACH] * values
    for shift in range(1, BLUR_REACH + 1):
        both = pltpu.roll(values, shift, 0) + pltpu.roll(values, rows - shift, 0)
        result = result + weights[BLUR_REACH + shift] * both
    return result


def profile_rows(coord, side, length, place, extent, slope):
    rows = length + 2 * PAD
    point = lax.broadcasted_iota(jnp.int32, (rows, coord.shape[-1]), 0) - PAD
    within = point + place * length
    start = side * length
    grid = (within >= 0) & (within < extent * length)
    window = grid & (point >= start - SPLAT_MARGIN) & (point < start + length + SPLAT_MARGIN)
    reach = grid & (point >= start - REACH) & (point < start + length + REACH)
    offset = jnp.asarray(side * length, jnp.float32)
    gap = point.astype(jnp.float32) - (coord + offset)
    plain = jnp.where(window, jnp.exp(-0.5 * gap * gap), 0.0)
    wide = jnp.where(reach, spread(plain), 0.0)
    if not slope:
        return wide
    return wide, jnp.where(reach, spread(gap * plain), 0.0)


def sort_kernel(own_ref, chunk_ref, column_ref, row_ref, rank_ref):
    slots = own_ref.shape[-1]
    own = own_ref[...]
    turned = own.T
    first = lax.broadcasted_iota(jnp.int32, (slots, slots), 0)
    second = lax.broadcasted_iota(jnp.int32, (slots, slots), 1)
    earlier = second < first
    far = 9.0e3
    part_row = jnp.zeros((1, slots), jnp.float32)
    part_column = jnp.zeros((slots, 1), jnp.float32)
    for axis, size in ((0, slots // 2), (1, LANES), (2, 1)):
        row = jnp.where(own[7:8, :] > 0.5, jnp.clip(own[axis : axis + 1, :], -5.0e3, 5.0e3), far)
        column = jnp.where(
            turned[:, 7:8] > 0.5, jnp.clip(turned[:, axis : axis + 1], -5.0e3, 5.0e3), far
        )
        row = row + 1.0e5 * part_row
        column = column + 1.0e5 * part_column
        before = jnp.where((row < column) | ((row == column) & earlier), 1.0, 0.0)
        rank_column = jnp.sum(before, axis=1, keepdims=True)
        rank_row = float(slots - 1) - jnp.sum(before, axis=0, keepdims=True)
        part_column = jnp.floor(rank_column * (1.0 / size))
        part_row = jnp.floor(rank_row * (1.0 / size))
    place = jnp.where(rank_column.astype(jnp.int32) == second, 1.0, 0.0)
    ordered = jnp.dot(
        own, place, precision=lax.Precision.HIGHEST, preferred_element_type=jnp.float32
    )
    row_ref[...] = ordered
    column_ref[...] = ordered.T
    for k in range(slots // LANES):
        chunk_ref[k] = ordered[:, k * LANES : (k + 1) * LANES]
    rank_ref[...] = rank_row.astype(jnp.int32)


def born_kernel(near_ref, own_ref, list_ref, count_ref, offset_ref, out_ref):
    slots = own_ref.shape[0]

    def block(index, carry):
        base = pl.multiple_of(index * ROWS, ROWS)
        own = [
            jnp.broadcast_to(own_ref[pl.ds(base, ROWS), k : k + 1], (ROWS, LANES))
            for k in range(3)
        ]

        def visit(step, summed):
            number = list_ref[index, step]
            squared = None
            for axis in range(3):
                row = near_ref[number, axis : axis + 1, :] + offset_ref[number, axis]
                gap = own[axis] - row
                squared = gap * gap if squared is None else squared + gap * gap
            smooth = jnp.maximum(1.0 - squared * (1.0 / (CUTOFF * CUTOFF)), 0.0)
            weight = near_ref[number, 4:5, :]
            return summed + jnp.exp(squared * -0.125) * (smooth * smooth) * weight

        summed = lax.fori_loop(
            0, count_ref[0, index], visit, jnp.zeros((ROWS, LANES), jnp.float32)
        )
        own_screen = own_ref[pl.ds(base, ROWS), 4:5]
        radius = own_ref[pl.ds(base, ROWS), 6:7]
        out_ref[pl.ds(base, ROWS), :] = radius + (
            jnp.sum(summed, axis=1, keepdims=True) - own_screen
        )
        return carry

    lax.fori_loop(0, slots // ROWS, block, 0)


def force_kernel(
    scale, near_ref, radii_ref, own_ref, radius_ref, fit_ref, rank_ref, list_ref, count_ref,
    offset_ref, out_ref, held_ref,
):
    slots = own_ref.shape[0]
    held_ref[...] = jnp.zeros_like(held_ref)

    def block(index, carry):
        base = pl.multiple_of(index * ROWS, ROWS)
        own = [
            jnp.broadcast_to(own_ref[pl.ds(base, ROWS), k : k + 1], (ROWS, LANES))
            for k in range(3)
        ]
        radius = jnp.broadcast_to(radius_ref[pl.ds(base, ROWS), :], (ROWS, LANES))
        inverse_radius = -0.25 / radius

        def visit(step, summed):
            number = list_ref[index, step]
            squared = None
            gaps = []
            for axis in range(3):
                row = near_ref[number, axis : axis + 1, :] + offset_ref[number, axis]
                gap = own[axis] - row
                gaps.append(gap)
                squared = gap * gap if squared is None else squared + gap * gap
            smooth = jnp.maximum(1.0 - squared * (1.0 / (CUTOFF * CUTOFF)), 0.0)
            near_radius = radii_ref[number]
            charge = near_ref[number, 3:4, :]
            fading = jnp.exp(squared * (inverse_radius * (1.0 / near_radius)))
            inverse = lax.rsqrt(squared + (radius * near_radius) * fading)
            common = (charge * (smooth * inverse)) * (
                2.0 / (CUTOFF * CUTOFF)
                + (smooth * (inverse * inverse)) * (0.5 - 0.125 * fading)
            )
            return tuple(total + common * gap for total, gap in zip(summed, gaps))

        zero = jnp.zeros((ROWS, LANES), jnp.float32)
        summed = lax.fori_loop(0, count_ref[0, index], visit, (zero, zero, zero))
        charge = own_ref[pl.ds(base, ROWS), 3:4]
        for axis in range(3):
            held_ref[pl.ds(base, ROWS), axis : axis + 1] = -charge * jnp.sum(
                summed[axis], axis=1, keepdims=True
            )
        return carry

    lax.fori_loop(0, slots // ROWS, block, 0)
    force = held_ref[...].T + scale * fit_ref[...]
    slot = lax.broadcasted_iota(jnp.int32, (slots, slots), 0)
    back = jnp.where(slot == rank_ref[...], 1.0, 0.0)
    out_ref[...] = jnp.dot(
        force, back, precision=lax.Precision.HIGHEST, preferred_element_type=jnp.float32
    )


def halves(value):
    high = value.astype(jnp.bfloat16)
    return high, (value - high.astype(jnp.float32)).astype(jnp.bfloat16)


def evolved_kernel(
    dims, sizes, near_ref, map_ref, place_ref, out_ref, part_ref, px_ref, py_ref, pz_ref, total_ref
):
    places = [place_ref[0, k] for k in range(3)]
    pieces = near_ref.shape[0] // 27
    depth = dims[2]

    def there(sides):
        inside = None
        for axis in range(3):
            spot = places[axis] + sides[axis]
            good = (spot >= 0) & (spot < sizes[axis])
            inside = good if inside is None else inside & good
        return inside

    def profiles(cell, carry):
        sides = sides_of(cell)

        @pl.when(there(sides))
        def _():
            for piece in range(pieces):
                atoms = near_ref.at[cell * pieces + piece]
                lanes = slice(piece * LANES, (piece + 1) * LANES)
                made = [
                    profile_rows(
                        atoms[axis : axis + 1, :],
                        sides[axis],
                        dims[axis],
                        places[axis],
                        sizes[axis],
                        False,
                    )[PAD : PAD + dims[axis]]
                    for axis in range(3)
                ]
                px_ref[cell, :, lanes] = made[0] * atoms[5:6, :]
                py_ref[cell, :, lanes] = made[1]
                high, low = halves(made[2])
                pz_ref[cell, 0:depth, lanes] = high
                pz_ref[cell, depth : 2 * depth, lanes] = low

        return carry

    lax.fori_loop(0, 27, profiles, 0)
    out_ref[...] = jnp.zeros_like(out_ref)
    spans_x = ((0, REACH), (0, dims[0]), (dims[0] - REACH, dims[0]))
    spans_y = ((0, PAD), (0, dims[1]), (dims[1] - PAD, dims[1]))
    for ix in range(3):
        for iy in range(3):
            x0, x1 = spans_x[ix]
            y0, y1 = spans_y[iy]
            rows = (x1 - x0) * (y1 - y0)

            @pl.when(there((ix - 1, iy - 1, 0)))
            def _(ix=ix, iy=iy, x0=x0, x1=x1, y0=y0, y1=y1, rows=rows):
                total_ref[0 : 2 * rows, :] = jnp.zeros((2 * rows, 2 * depth), jnp.float32)

                def add(iz, carry):
                    cell = ix * 9 + iy * 3 + iz

                    @pl.when(there((ix - 1, iy - 1, iz - 1)))
                    def _():
                        py = py_ref[cell, y0:y1, :]
                        pieces_high, pieces_low = [], []
                        for k in range(x0, x1):
                            value = px_ref[cell, k : k + 1, :] * py
                            upper = value.astype(jnp.bfloat16).astype(jnp.float32)
                            pieces_high.append(upper)
                            pieces_low.append(value - upper)
                        plane = jnp.concatenate(pieces_high + pieces_low, axis=0)
                        total_ref[0 : 2 * rows, :] += lax.dot_general(
                            plane.astype(jnp.bfloat16),
                            pz_ref[cell],
                            (((1,), (1,)), ((), ())),
                            preferred_element_type=jnp.float32,
                        )

                    return carry

                lax.fori_loop(0, 3, add, 0)
                result = (
                    total_ref[0:rows, 0:depth]
                    + total_ref[0:rows, depth : 2 * depth]
                    + total_ref[rows : 2 * rows, 0:depth]
                )
                out_ref[x0:x1, y0:y1, :] += result.reshape(x1 - x0, y1 - y0, depth)

    evolved = out_ref[...]
    given = map_ref[...]
    lane = lax.broadcasted_iota(jnp.int32, (1, LANES), 1)
    part_ref[...] = jnp.where(
        lane == 0,
        jnp.sum(evolved * evolved),
        jnp.where(
            lane == 1,
            jnp.sum(evolved * given),
            jnp.where(lane == 2, jnp.sum(given * given), 0.0),
        ),
    )


def fit_kernel(dims, sizes, own_ref, place_ref, sens_ref, out_ref, big_ref):
    places = [place_ref[0, k] for k in range(3)]
    slots = own_ref.shape[-1]
    wide = []
    slope = []
    for axis in range(3):
        a, b = profile_rows(
            own_ref[axis : axis + 1, :], 0, dims[axis], places[axis], sizes[axis], True
        )
        wide.append(a)
        slope.append(b)
    both = jnp.concatenate([wide[2], slope[2]], axis=1)
    high, low = halves(both)
    right = jnp.concatenate([high, low, high], axis=0)
    big_ref[...] = jnp.dot(sens_ref[...], right, preferred_element_type=jnp.float32)
    height = dims[1] + 2 * PAD
    force = [jnp.zeros((1, slots), jnp.float32) for _ in range(3)]
    for k in range(dims[0] + 2 * REACH):
        row = PAD - REACH + k
        plain_z = big_ref[k * height : (k + 1) * height, 0:slots]
        slope_z = big_ref[k * height : (k + 1) * height, slots : 2 * slots]
        plain = jnp.sum(plain_z * wide[1], axis=0, keepdims=True)
        turned_y = jnp.sum(plain_z * slope[1], axis=0, keepdims=True)
        turned_z = jnp.sum(slope_z * wide[1], axis=0, keepdims=True)
        here = wide[0][row : row + 1, :]
        force[0] = force[0] + slope[0][row : row + 1, :] * plain
        force[1] = force[1] + here * turned_y
        force[2] = force[2] + here * turned_z
    mass = own_ref[5:6, :]
    out_ref[...] = jnp.zeros_like(out_ref)
    for axis in range(3):
        out_ref[axis : axis + 1, :] = mass * force[axis]


def frame_map(bricks, dims):
    reaches = (REACH, PAD, PAD)
    cube = bricks.reshape((3, 3, 3) + dims)

    def join(parts, axis):
        length = dims[axis]
        return jnp.concatenate(
            [
                lax.slice_in_dim(parts[0], length - reaches[axis], length, axis=axis),
                parts[1],
                lax.slice_in_dim(parts[2], 0, reaches[axis], axis=axis),
            ],
            axis=axis,
        )

    return join(
        [join([join([cube[a, b, c] for c in range(3)], 2) for b in range(3)], 1) for a in range(3)],
        0,
    )


def active_lists(near, columns, offsets):
    whole = near.shape[0]
    slots = columns.shape[0]
    blocks = slots // ROWS
    coords = near[:, 0:3, :] + offsets[:, :, None]
    live = near[:, 7:8, :] > 0.5
    big = 1e30
    low = jnp.where(live, coords, big).min(axis=-1)
    high = jnp.where(live, coords, -big).max(axis=-1)
    grouped = columns.reshape(blocks, ROWS, columns.shape[1])
    own_live = grouped[:, :, 7:8] > 0.5
    own_low = jnp.where(own_live, grouped[:, :, 0:3], big).min(axis=1)
    own_high = jnp.where(own_live, grouped[:, :, 0:3], -big).max(axis=1)
    apart = jnp.maximum(
        low[None, :, :] - own_high[:, None, :], own_low[:, None, :] - high[None, :, :]
    )
    apart = jnp.maximum(apart, 0.0)
    keep = jnp.sum(apart * apart, axis=-1) < CUTOFF * CUTOFF * 1.001
    index = jnp.arange(whole, dtype=jnp.int32)
    before = (index[:, None] <= index[None, :]).astype(jnp.bfloat16)
    spot = jnp.dot(
        keep.astype(jnp.bfloat16), before, preferred_element_type=jnp.float32
    ).astype(jnp.int32)
    counts = spot[:, -1]
    chosen = keep[:, :, None] & (spot[:, :, None] - 1 == index[None, None, :])
    lists = jnp.sum(jnp.where(chosen, index[None, :, None], 0), axis=1)
    return lists, counts[None, :]


def on_device(positions, charges, atom_types, type_table, live_count, exp_map):
    dims = exp_map.shape
    sizes = tuple(lax.axis_size(axis) for axis in AXES)
    slots = positions.shape[-1]
    grid_points = dims[0] * dims[1] * dims[2] * sizes[0] * sizes[1] * sizes[2]
    scale = FIT_GAIN * float(grid_points)
    place = jnp.stack([lax.axis_index(axis) for axis in AXES]).astype(jnp.int32).reshape(1, 3)

    kinds = jnp.arange(type_table.shape[1], dtype=jnp.int32)
    onehot = (atom_types.reshape(1, slots) == kinds[:, None]).astype(jnp.float32)
    props = jnp.sum(type_table[:, :, None] * onehot[None], axis=1)
    living = (
        lax.broadcasted_iota(jnp.int32, (1, slots), 1) < live_count.reshape(1, 1)
    ).astype(jnp.float32)
    start = positions.reshape(3, slots)
    fixed = jnp.concatenate(
        [
            charges.reshape(1, slots) * living,
            props[1:2] * living,
            props[2:3] * living,
            props[0:1],
            living,
        ],
        axis=0,
    )
    current = start
    pieces = slots // LANES
    number = jnp.arange(27 * pieces, dtype=jnp.int32) // pieces
    offsets = jnp.stack(sides_of(number), axis=1).astype(jnp.float32) * jnp.array(
        dims, jnp.float32
    )
    framed = None
    for step in range(STEPS):
        own = jnp.concatenate([current, fixed], axis=0)
        chunks, columns, ordered, rank = pl.pallas_call(
            sort_kernel,
            out_shape=[
                jax.ShapeDtypeStruct((pieces, 8, LANES), jnp.float32),
                jax.ShapeDtypeStruct((slots, 8), jnp.float32),
                jax.ShapeDtypeStruct((8, slots), jnp.float32),
                jax.ShapeDtypeStruct((1, slots), jnp.int32),
            ],
            in_specs=[VMEM],
            out_specs=[VMEM] * 4,
            name="sort",
        )(own)
        if step == 0:
            near, bricks = exchange([chunks, exp_map.reshape(-1, LANES)], None, 0)
            framed = frame_map(bricks, dims)
        else:
            (near,) = exchange([chunks], None, 1)
        near = near.reshape(27 * pieces, 8, LANES)
        lists, counts = active_lists(near, columns, offsets)
        radius = pl.pallas_call(
            born_kernel,
            out_shape=jax.ShapeDtypeStruct((slots, 1), jnp.float32),
            in_specs=[VMEM, VMEM, SMEM, SMEM, SMEM],
            out_specs=VMEM,
            name="born",
        )(near, columns, lists, counts, offsets)
        evolved, part = pl.pallas_call(
            functools.partial(evolved_kernel, dims, sizes),
            out_shape=[
                jax.ShapeDtypeStruct(dims, jnp.float32),
                jax.ShapeDtypeStruct((1, LANES), jnp.float32),
            ],
            in_specs=[VMEM, VMEM, SMEM],
            out_specs=[VMEM, VMEM],
            scratch_shapes=[
                pltpu.VMEM((27, dims[0], slots), jnp.float32),
                pltpu.VMEM((27, dims[1], slots), jnp.float32),
                pltpu.VMEM((27, 2 * dims[2], slots), jnp.bfloat16),
                pltpu.VMEM((2 * dims[0] * dims[1], 2 * dims[2]), jnp.float32),
            ],
            name="evolve",
        )(near, exp_map, place)
        near_radius, halo, parts = exchange(
            [radius.reshape(pieces, 1, LANES), evolved.reshape(-1, LANES)], part, 2
        )
        near_radius = near_radius.reshape(27 * pieces, 1, LANES)
        wide = frame_map(halo, dims)
        sums = jnp.sum(parts, axis=(0, 1))
        squares, cross_sum, whole_target = sums[0], sums[1], sums[2]
        norm = jnp.sqrt((squares + EPSILON) * (whole_target + EPSILON))
        score = cross_sum / norm
        sensitivity = framed / norm - score * wide / (squares + EPSILON)
        sensitivity = sensitivity.reshape(-1, sensitivity.shape[-1])
        rounded = lax.reduce_precision(sensitivity, 8, 7)
        high, low = rounded.astype(jnp.bfloat16), (sensitivity - rounded).astype(jnp.bfloat16)
        stacked = jnp.concatenate([high, high, low], axis=1)
        fit = pl.pallas_call(
            functools.partial(fit_kernel, dims, sizes),
            out_shape=jax.ShapeDtypeStruct((8, slots), jnp.float32),
            in_specs=[VMEM, SMEM, VMEM],
            out_specs=VMEM,
            scratch_shapes=[pltpu.VMEM((stacked.shape[0], 2 * slots), jnp.float32)],
            name="fit",
        )(ordered, place, stacked)
        force = pl.pallas_call(
            functools.partial(force_kernel, scale),
            out_shape=jax.ShapeDtypeStruct((8, slots), jnp.float32),
            in_specs=[VMEM] * 6 + [SMEM] * 3,
            out_specs=VMEM,
            scratch_shapes=[pltpu.VMEM((slots, 8), jnp.float32)],
            name="pair",
        )(near, near_radius, columns, radius, fit, rank, lists, counts, offsets)[0:3]
        current = current + STEP_SIZE * (living * force)
    shape = positions.shape
    return ((current - start).reshape(shape), force.reshape(shape), evolved)


def solution(mesh):
    placed = (
        P(None, "gx", "gy", "gz", None),
        P("gx", "gy", "gz", None),
        P("gx", "gy", "gz", None),
        P(),
        P("gx", "gy", "gz"),
        P("gx", "gy", "gz"),
    )
    return jax.shard_map(
        on_device,
        mesh=mesh,
        in_specs=placed,
        out_specs=(
            P(None, "gx", "gy", "gz", None),
            P(None, "gx", "gy", "gz", None),
            P("gx", "gy", "gz"),
        ),
        check_vma=False,
    )
```

```python
import functools
import math

import jax
import jax.numpy as jnp
from jax import lax
from jax.experimental import pallas as pl
from jax.experimental.pallas import tpu as pltpu
from jax.sharding import PartitionSpec as P

SPLAT_MARGIN = 3
BLUR_REACH = 2
STEPS = 2
CUTOFF = 10.0
EPSILON = 1e-06
STEP_SIZE = 1.0
FIT_GAIN = 0.2
REACH = SPLAT_MARGIN + BLUR_REACH
PAD = 8
LANES = 128
ROWS = 64
MESH = pl.DeviceIdType.MESH
AXES = ("gx", "gy", "gz")
VMEM = pl.BlockSpec(memory_space=pltpu.VMEM)
SMEM = pl.BlockSpec(memory_space=pltpu.SMEM)


def sides_of(number):
    return (number // 9 - 1, number // 3 % 3 - 1, number % 3 - 1)


def exchange_kernel(sizes, count, everyone, *refs):
    sources = refs[:count]
    position = count
    if everyone:
        part_ref = refs[position]
        position += 1
    outs = refs[position : position + count]
    position += count
    if everyone:
        parts_out = refs[position]
        position += 1
    send, recv = refs[position : position + 2]
    me = tuple(lax.axis_index(axis) for axis in AXES)
    total = sizes[0] * sizes[1] * sizes[2]
    mine = (me[0] * sizes[1] + me[1]) * sizes[2] + me[2]

    def exists(number):
        sides = sides_of(number)
        inside = None
        for axis in range(3):
            place = me[axis] + sides[axis]
            good = (place >= 0) & (place < sizes[axis])
            inside = good if inside is None else inside & good
        return inside

    def target(number):
        sides = sides_of(number)
        return tuple(me[axis] + sides[axis] for axis in range(3))

    def device_at(linear):
        return (
            linear // (sizes[1] * sizes[2]),
            linear // sizes[2] % sizes[1],
            linear % sizes[2],
        )

    others = [number for number in range(27) if number != 13]
    barrier = pltpu.get_barrier_semaphore()
    if everyone:

        def greet(step, carry):
            linear = lax.rem(mine + step, total)
            pl.semaphore_signal(barrier, inc=1, device_id=device_at(linear), device_id_type=MESH)
            return carry

        lax.fori_loop(1, total, greet, 0)
        pl.semaphore_wait(barrier, total - 1)
        send_all, recv_all = refs[position + 2 : position + 4]
    else:
        expected = 1
        for axis in range(3):
            low = jnp.where(me[axis] > 0, 1, 0)
            high = jnp.where(me[axis] < sizes[axis] - 1, 1, 0)
            expected = expected * (1 + low + high)
        for number in others:

            @pl.when(exists(number))
            def _(number=number):
                pl.semaphore_signal(barrier, inc=1, device_id=target(number), device_id_type=MESH)

        pl.semaphore_wait(barrier, expected - 1)

    def outgoing(index, number):
        return pltpu.make_async_remote_copy(
            src_ref=sources[index],
            dst_ref=outs[index].at[26 - number],
            send_sem=send.at[index, number],
            recv_sem=recv.at[index, 26 - number],
            device_id=target(number),
            device_id_type=MESH,
        )

    def arriving(index, number):
        return pltpu.make_async_remote_copy(
            src_ref=sources[index],
            dst_ref=outs[index].at[number],
            send_sem=send.at[index, number],
            recv_sem=recv.at[index, number],
            device_id=target(number),
            device_id_type=MESH,
        )

    def sum_copy(linear, slot):
        return pltpu.make_async_remote_copy(
            src_ref=part_ref,
            dst_ref=parts_out.at[slot],
            send_sem=send_all.at[linear],
            recv_sem=recv_all.at[slot],
            device_id=device_at(linear),
            device_id_type=MESH,
        )

    if everyone:

        def send_sum(step, carry):
            sum_copy(lax.rem(mine + step, total), mine).start()
            return carry

        lax.fori_loop(1, total, send_sum, 0)
    for number in others:

        @pl.when(exists(number))
        def _(number=number):
            for index in range(count):
                outgoing(index, number).start()

    for index in range(count):
        outs[index][13] = sources[index][...]
    if everyone:
        parts_out[mine] = part_ref[...]
    for number in others:

        @pl.when(jnp.logical_not(exists(number)))
        def _(number=number):
            for index in range(count):
                outs[index][number] = jnp.zeros(sources[index].shape, jnp.float32)

    for number in others:

        @pl.when(exists(number))
        def _(number=number):
            for index in range(count):
                outgoing(index, number).wait_send()
                arriving(index, number).wait_recv()

    if everyone:

        def wait_sum(step, carry):
            linear = lax.rem(mine + step, total)
            sum_copy(linear, mine).wait_send()
            sum_copy(linear, linear).wait_recv()
            return carry

        lax.fori_loop(1, total, wait_sum, 0)


def exchange(arrays, part, collective_id):
    sizes = tuple(lax.axis_size(axis) for axis in AXES)
    total = sizes[0] * sizes[1] * sizes[2]
    count = len(arrays)
    everyone = part is not None
    out_shape = [jax.ShapeDtypeStruct((27,) + a.shape, jnp.float32) for a in arrays]
    scratch = [pltpu.SemaphoreType.DMA((count, 27)), pltpu.SemaphoreType.DMA((count, 27))]
    operands = list(arrays)
    if everyone:
        operands.append(part)
        out_shape.append(jax.ShapeDtypeStruct((total,) + part.shape, jnp.float32))
        scratch += [pltpu.SemaphoreType.DMA((total,)), pltpu.SemaphoreType.DMA((total,))]
    return pl.pallas_call(
        functools.partial(exchange_kernel, sizes, count, everyone),
        out_shape=out_shape,
        in_specs=[VMEM] * len(operands),
        out_specs=[VMEM] * len(out_shape),
        scratch_shapes=scratch,
        compiler_params=pltpu.CompilerParams(collective_id=collective_id, has_side_effects=True),
        name=f"exchange{collective_id}",
    )(*operands)


def kernel_weights(reach):
    values = [math.exp(-0.5 * (index - reach) ** 2) for index in range(2 * reach + 1)]
    whole = sum(values)
    return [value / whole for value in values]


def spread(values):
    weights = kernel_weights(BLUR_REACH)
    rows = values.shape[0]
    result = weights[BLUR_REACH] * values
    for shift in range(1, BLUR_REACH + 1):
        both = pltpu.roll(values, shift, 0) + pltpu.roll(values, rows - shift, 0)
        result = result + weights[BLUR_REACH + shift] * both
    return result


def profile_rows(coord, side, length, place, extent, slope):
    rows = length + 2 * PAD
    point = lax.broadcasted_iota(jnp.int32, (rows, coord.shape[-1]), 0) - PAD
    within = point + place * length
    start = side * length
    grid = (within >= 0) & (within < extent * length)
    window = grid & (point >= start - SPLAT_MARGIN) & (point < start + length + SPLAT_MARGIN)
    reach = grid & (point >= start - REACH) & (point < start + length + REACH)
    offset = jnp.asarray(side * length, jnp.float32)
    gap = point.astype(jnp.float32) - (coord + offset)
    plain = jnp.where(window, jnp.exp(-0.5 * gap * gap), 0.0)
    wide = jnp.where(reach, spread(plain), 0.0)
    if not slope:
        return wide
    return wide, jnp.where(reach, spread(gap * plain), 0.0)


def move(values, onehot):
    rows = values.shape[0]
    first = values.astype(jnp.bfloat16).astype(jnp.float32)
    rest = values - first
    second = rest.astype(jnp.bfloat16).astype(jnp.float32)
    stacked = jnp.concatenate([first, second, rest - second], axis=0).astype(jnp.bfloat16)
    moved = jnp.dot(stacked, onehot.astype(jnp.bfloat16), preferred_element_type=jnp.float32)
    return moved[0:rows] + (moved[rows : 2 * rows] + moved[2 * rows : 3 * rows])


def sort_kernel(own_ref, chunk_ref, column_ref, row_ref, rank_ref):
    slots = own_ref.shape[-1]
    own = own_ref[...]
    turned = own.T
    first = lax.broadcasted_iota(jnp.int32, (slots, slots), 0)
    second = lax.broadcasted_iota(jnp.int32, (slots, slots), 1)
    earlier = second < first
    far = 9.0e3
    part_row = jnp.zeros((1, slots), jnp.float32)
    part_column = jnp.zeros((slots, 1), jnp.float32)
    for axis, size in ((0, slots // 2), (1, LANES), (2, 1)):
        row = jnp.where(own[7:8, :] > 0.5, jnp.clip(own[axis : axis + 1, :], -5.0e3, 5.0e3), far)
        column = jnp.where(
            turned[:, 7:8] > 0.5, jnp.clip(turned[:, axis : axis + 1], -5.0e3, 5.0e3), far
        )
        row = row + 1.0e5 * part_row
        column = column + 1.0e5 * part_column
        before = jnp.where((row < column) | ((row == column) & earlier), 1.0, 0.0)
        rank_column = jnp.sum(before, axis=1, keepdims=True)
        rank_row = float(slots - 1) - jnp.sum(before, axis=0, keepdims=True)
        part_column = jnp.floor(rank_column * (1.0 / size))
        part_row = jnp.floor(rank_row * (1.0 / size))
    place = jnp.where(rank_column.astype(jnp.int32) == second, 1.0, 0.0)
    ordered = move(own, place)
    row_ref[...] = ordered
    column_ref[...] = ordered.T
    for k in range(slots // LANES):
        chunk_ref[k] = ordered[:, k * LANES : (k + 1) * LANES]
    rank_ref[...] = rank_row.astype(jnp.int32)


def born_kernel(
    near_ref, own_ref, list_ref, count_ref, offset_ref, out_ref, row_ref, held_ref
):
    slots = own_ref.shape[0]
    held_ref[...] = jnp.zeros_like(held_ref)

    def block(index, carry):
        base = pl.multiple_of(index * ROWS, ROWS)
        own = [
            jnp.broadcast_to(own_ref[pl.ds(base, ROWS), k : k + 1], (ROWS, LANES))
            for k in range(3)
        ]

        def visit(step, summed):
            number = list_ref[index, step]
            squared = None
            for axis in range(3):
                row = near_ref[number, axis : axis + 1, :] + offset_ref[number, axis]
                gap = own[axis] - row
                squared = gap * gap if squared is None else squared + gap * gap
            smooth = jnp.maximum(1.0 - squared * (1.0 / (CUTOFF * CUTOFF)), 0.0)
            weight = near_ref[number, 4:5, :]
            return summed + jnp.exp(squared * -0.125) * (smooth * smooth) * weight

        summed = lax.fori_loop(
            0, count_ref[0, index], visit, jnp.zeros((ROWS, LANES), jnp.float32)
        )
        own_screen = own_ref[pl.ds(base, ROWS), 4:5]
        radius = own_ref[pl.ds(base, ROWS), 6:7]
        found = radius + (jnp.sum(summed, axis=1, keepdims=True) - own_screen)
        out_ref[pl.ds(base, ROWS), :] = found
        held_ref[pl.ds(base, ROWS), 0:1] = found
        return carry

    lax.fori_loop(0, slots // ROWS, block, 0)
    turned = held_ref[...].T
    for piece in range(slots // LANES):
        row_ref[piece] = turned[0:1, piece * LANES : (piece + 1) * LANES]


def force_kernel(
    scale, near_ref, radii_ref, own_ref, radius_ref, fit_ref, rank_ref, list_ref, count_ref,
    offset_ref, out_ref, held_ref,
):
    slots = own_ref.shape[0]
    held_ref[...] = jnp.zeros_like(held_ref)

    def block(index, carry):
        base = pl.multiple_of(index * ROWS, ROWS)
        own = [
            jnp.broadcast_to(own_ref[pl.ds(base, ROWS), k : k + 1], (ROWS, LANES))
            for k in range(3)
        ]
        radius = jnp.broadcast_to(radius_ref[pl.ds(base, ROWS), :], (ROWS, LANES))
        inverse_radius = -0.25 / radius

        def visit(step, summed):
            number = list_ref[index, step]
            squared = None
            gaps = []
            for axis in range(3):
                row = near_ref[number, axis : axis + 1, :] + offset_ref[number, axis]
                gap = own[axis] - row
                gaps.append(gap)
                squared = gap * gap if squared is None else squared + gap * gap
            smooth = jnp.maximum(1.0 - squared * (1.0 / (CUTOFF * CUTOFF)), 0.0)
            near_radius = radii_ref[number]
            charge = near_ref[number, 3:4, :]
            fading = jnp.exp(squared * (inverse_radius * (1.0 / near_radius)))
            inverse = lax.rsqrt(squared + (radius * near_radius) * fading)
            common = (charge * (smooth * inverse)) * (
                2.0 / (CUTOFF * CUTOFF)
                + (smooth * (inverse * inverse)) * (0.5 - 0.125 * fading)
            )
            return tuple(total + common * gap for total, gap in zip(summed, gaps))

        zero = jnp.zeros((ROWS, LANES), jnp.float32)
        summed = lax.fori_loop(0, count_ref[0, index], visit, (zero, zero, zero))
        charge = own_ref[pl.ds(base, ROWS), 3:4]
        for axis in range(3):
            held_ref[pl.ds(base, ROWS), axis : axis + 1] = -charge * jnp.sum(
                summed[axis], axis=1, keepdims=True
            )
        return carry

    lax.fori_loop(0, slots // ROWS, block, 0)
    force = held_ref[...].T + scale * fit_ref[...]
    slot = lax.broadcasted_iota(jnp.int32, (slots, slots), 0)
    back = jnp.where(slot == rank_ref[...], 1.0, 0.0)
    out_ref[...] = move(force, back)


def halves(value):
    high = value.astype(jnp.bfloat16)
    return high, (value - high.astype(jnp.float32)).astype(jnp.bfloat16)


def evolved_kernel(
    dims, sizes, near_ref, map_ref, place_ref, out_ref, part_ref, px_ref, py_ref, pz_ref, total_ref
):
    places = [place_ref[0, k] for k in range(3)]
    pieces = near_ref.shape[0] // 27
    depth = dims[2]

    def there(sides):
        inside = None
        for axis in range(3):
            spot = places[axis] + sides[axis]
            good = (spot >= 0) & (spot < sizes[axis])
            inside = good if inside is None else inside & good
        return inside

    def profiles(cell, carry):
        sides = sides_of(cell)

        @pl.when(there(sides))
        def _():
            for piece in range(pieces):
                atoms = near_ref.at[cell * pieces + piece]
                lanes = slice(piece * LANES, (piece + 1) * LANES)
                made = [
                    profile_rows(
                        atoms[axis : axis + 1, :],
                        sides[axis],
                        dims[axis],
                        places[axis],
                        sizes[axis],
                        False,
                    )[PAD : PAD + dims[axis]]
                    for axis in range(3)
                ]
                px_ref[cell, :, lanes] = made[0] * atoms[5:6, :]
                py_ref[cell, :, lanes] = made[1]
                high, low = halves(made[2])
                pz_ref[cell, 0:depth, lanes] = high
                pz_ref[cell, depth : 2 * depth, lanes] = low

        return carry

    lax.fori_loop(0, 27, profiles, 0)
    out_ref[...] = jnp.zeros_like(out_ref)
    spans_x = ((0, REACH), (0, dims[0]), (dims[0] - REACH, dims[0]))
    spans_y = ((0, PAD), (0, dims[1]), (dims[1] - PAD, dims[1]))
    for ix in range(3):
        for iy in range(3):
            x0, x1 = spans_x[ix]
            y0, y1 = spans_y[iy]
            rows = (x1 - x0) * (y1 - y0)

            @pl.when(there((ix - 1, iy - 1, 0)))
            def _(ix=ix, iy=iy, x0=x0, x1=x1, y0=y0, y1=y1, rows=rows):
                total_ref[0 : 2 * rows, :] = jnp.zeros((2 * rows, 2 * depth), jnp.float32)

                def add(iz, carry):
                    cell = ix * 9 + iy * 3 + iz

                    @pl.when(there((ix - 1, iy - 1, iz - 1)))
                    def _():
                        py = py_ref[cell, y0:y1, :]
                        pieces_high, pieces_low = [], []
                        for k in range(x0, x1):
                            value = px_ref[cell, k : k + 1, :] * py
                            upper = value.astype(jnp.bfloat16).astype(jnp.float32)
                            pieces_high.append(upper)
                            pieces_low.append(value - upper)
                        plane = jnp.concatenate(pieces_high + pieces_low, axis=0)
                        total_ref[0 : 2 * rows, :] += lax.dot_general(
                            plane.astype(jnp.bfloat16),
                            pz_ref[cell],
                            (((1,), (1,)), ((), ())),
                            preferred_element_type=jnp.float32,
                        )

                    return carry

                lax.fori_loop(0, 3, add, 0)
                result = (
                    total_ref[0:rows, 0:depth]
                    + total_ref[0:rows, depth : 2 * depth]
                    + total_ref[rows : 2 * rows, 0:depth]
                )
                out_ref[x0:x1, y0:y1, :] += result.reshape(x1 - x0, y1 - y0, depth)

    evolved = out_ref[...]
    given = map_ref[...]
    lane = lax.broadcasted_iota(jnp.int32, (1, LANES), 1)
    part_ref[...] = jnp.where(
        lane == 0,
        jnp.sum(evolved * evolved),
        jnp.where(
            lane == 1,
            jnp.sum(evolved * given),
            jnp.where(lane == 2, jnp.sum(given * given), 0.0),
        ),
    )


def fit_kernel(dims, sizes, own_ref, place_ref, sens_ref, out_ref, big_ref):
    places = [place_ref[0, k] for k in range(3)]
    slots = own_ref.shape[-1]
    wide = []
    slope = []
    for axis in range(3):
        a, b = profile_rows(
            own_ref[axis : axis + 1, :], 0, dims[axis], places[axis], sizes[axis], True
        )
        wide.append(a)
        slope.append(b)
    both = jnp.concatenate([wide[2], slope[2]], axis=1)
    high, low = halves(both)
    right = jnp.concatenate([high, low, high], axis=0)
    big_ref[...] = jnp.dot(sens_ref[...], right, preferred_element_type=jnp.float32)
    height = dims[1] + 2 * PAD
    force = [jnp.zeros((1, slots), jnp.float32) for _ in range(3)]
    for k in range(dims[0] + 2 * REACH):
        row = PAD - REACH + k
        plain_z = big_ref[k * height : (k + 1) * height, 0:slots]
        slope_z = big_ref[k * height : (k + 1) * height, slots : 2 * slots]
        plain = jnp.sum(plain_z * wide[1], axis=0, keepdims=True)
        turned_y = jnp.sum(plain_z * slope[1], axis=0, keepdims=True)
        turned_z = jnp.sum(slope_z * wide[1], axis=0, keepdims=True)
        here = wide[0][row : row + 1, :]
        force[0] = force[0] + slope[0][row : row + 1, :] * plain
        force[1] = force[1] + here * turned_y
        force[2] = force[2] + here * turned_z
    mass = own_ref[5:6, :]
    out_ref[...] = jnp.zeros_like(out_ref)
    for axis in range(3):
        out_ref[axis : axis + 1, :] = mass * force[axis]


def frame_kernel(dims, cube_ref, out_ref):
    reaches = (REACH, PAD, PAD)

    def span(side, axis):
        length, reach = dims[axis], reaches[axis]
        if side == 0:
            return slice(length - reach, length), slice(0, reach)
        if side == 1:
            return slice(0, length), slice(reach, reach + length)
        return slice(0, reach), slice(reach + length, length + 2 * reach)

    for a in range(3):
        from_x, to_x = span(a, 0)
        for b in range(3):
            from_y, to_y = span(b, 1)
            out_ref[to_x, to_y, :] = jnp.concatenate(
                [
                    cube_ref[a * 9 + b * 3 + c, from_x, from_y, :][:, :, span(c, 2)[0]]
                    for c in range(3)
                ],
                axis=2,
            )


def frame_map(bricks, dims):
    return pl.pallas_call(
        functools.partial(frame_kernel, dims),
        out_shape=jax.ShapeDtypeStruct(
            (dims[0] + 2 * REACH, dims[1] + 2 * PAD, dims[2] + 2 * PAD), jnp.float32
        ),
        in_specs=[VMEM],
        out_specs=VMEM,
        name="frame",
    )(bricks.reshape((27,) + dims))


def active_lists(near, columns, offsets):
    whole = near.shape[0]
    slots = columns.shape[0]
    blocks = slots // ROWS
    coords = near[:, 0:3, :] + offsets[:, :, None]
    live = near[:, 7:8, :] > 0.5
    big = 1e30
    low = jnp.where(live, coords, big).min(axis=-1)
    high = jnp.where(live, coords, -big).max(axis=-1)
    grouped = columns.reshape(blocks, ROWS, columns.shape[1])
    own_live = grouped[:, :, 7:8] > 0.5
    own_low = jnp.where(own_live, grouped[:, :, 0:3], big).min(axis=1)
    own_high = jnp.where(own_live, grouped[:, :, 0:3], -big).max(axis=1)
    apart = jnp.maximum(
        low[None, :, :] - own_high[:, None, :], own_low[:, None, :] - high[None, :, :]
    )
    apart = jnp.maximum(apart, 0.0)
    keep = jnp.sum(apart * apart, axis=-1) < CUTOFF * CUTOFF * 1.001
    index = jnp.arange(whole, dtype=jnp.int32)
    before = (index[:, None] <= index[None, :]).astype(jnp.bfloat16)
    spot = jnp.dot(
        keep.astype(jnp.bfloat16), before, preferred_element_type=jnp.float32
    ).astype(jnp.int32)
    counts = spot[:, -1]
    chosen = keep[:, :, None] & (spot[:, :, None] - 1 == index[None, None, :])
    lists = jnp.sum(jnp.where(chosen, index[None, :, None], 0), axis=1)
    return lists, counts[None, :]


def on_device(positions, charges, atom_types, type_table, live_count, exp_map):
    dims = exp_map.shape
    sizes = tuple(lax.axis_size(axis) for axis in AXES)
    slots = positions.shape[-1]
    grid_points = dims[0] * dims[1] * dims[2] * sizes[0] * sizes[1] * sizes[2]
    scale = FIT_GAIN * float(grid_points)
    place = jnp.stack([lax.axis_index(axis) for axis in AXES]).astype(jnp.int32).reshape(1, 3)

    kinds = jnp.arange(type_table.shape[1], dtype=jnp.int32)
    onehot = (atom_types.reshape(1, slots) == kinds[:, None]).astype(jnp.float32)
    props = jnp.sum(type_table[:, :, None] * onehot[None], axis=1)
    living = (
        lax.broadcasted_iota(jnp.int32, (1, slots), 1) < live_count.reshape(1, 1)
    ).astype(jnp.float32)
    start = positions.reshape(3, slots)
    fixed = jnp.concatenate(
        [
            charges.reshape(1, slots) * living,
            props[1:2] * living,
            props[2:3] * living,
            props[0:1],
            living,
        ],
        axis=0,
    )
    current = start
    pieces = slots // LANES
    number = jnp.arange(27 * pieces, dtype=jnp.int32) // pieces
    offsets = jnp.stack(sides_of(number), axis=1).astype(jnp.float32) * jnp.array(
        dims, jnp.float32
    )
    framed = None
    for step in range(STEPS):
        own = jnp.concatenate([current, fixed], axis=0)
        chunks, columns, ordered, rank = pl.pallas_call(
            sort_kernel,
            out_shape=[
                jax.ShapeDtypeStruct((pieces, 8, LANES), jnp.float32),
                jax.ShapeDtypeStruct((slots, 8), jnp.float32),
                jax.ShapeDtypeStruct((8, slots), jnp.float32),
                jax.ShapeDtypeStruct((1, slots), jnp.int32),
            ],
            in_specs=[VMEM],
            out_specs=[VMEM] * 4,
            name="sort",
        )(own)
        if step == 0:
            near, bricks = exchange([chunks, exp_map.reshape(-1, LANES)], None, 0)
            framed = frame_map(bricks, dims)
        else:
            (near,) = exchange([chunks], None, 1)
        near = near.reshape(27 * pieces, 8, LANES)
        lists, counts = active_lists(near, columns, offsets)
        radius, radius_rows = pl.pallas_call(
            born_kernel,
            out_shape=[
                jax.ShapeDtypeStruct((slots, 1), jnp.float32),
                jax.ShapeDtypeStruct((pieces, 1, LANES), jnp.float32),
            ],
            in_specs=[VMEM, VMEM, SMEM, SMEM, SMEM],
            out_specs=[VMEM, VMEM],
            scratch_shapes=[pltpu.VMEM((slots, 8), jnp.float32)],
            name="born",
        )(near, columns, lists, counts, offsets)
        evolved, part = pl.pallas_call(
            functools.partial(evolved_kernel, dims, sizes),
            out_shape=[
                jax.ShapeDtypeStruct(dims, jnp.float32),
                jax.ShapeDtypeStruct((1, LANES), jnp.float32),
            ],
            in_specs=[VMEM, VMEM, SMEM],
            out_specs=[VMEM, VMEM],
            scratch_shapes=[
                pltpu.VMEM((27, dims[0], slots), jnp.float32),
                pltpu.VMEM((27, dims[1], slots), jnp.float32),
                pltpu.VMEM((27, 2 * dims[2], slots), jnp.bfloat16),
                pltpu.VMEM((2 * dims[0] * dims[1], 2 * dims[2]), jnp.float32),
            ],
            name="evolve",
        )(near, exp_map, place)
        near_radius, halo, parts = exchange(
            [radius_rows, evolved.reshape(-1, LANES)], part, 2
        )
        near_radius = near_radius.reshape(27 * pieces, 1, LANES)
        wide = frame_map(halo, dims)
        sums = jnp.sum(parts, axis=(0, 1))
        squares, cross_sum, whole_target = sums[0], sums[1], sums[2]
        norm = jnp.sqrt((squares + EPSILON) * (whole_target + EPSILON))
        score = cross_sum / norm
        sensitivity = framed / norm - score * wide / (squares + EPSILON)
        sensitivity = sensitivity.reshape(-1, sensitivity.shape[-1])
        rounded = lax.reduce_precision(sensitivity, 8, 7)
        high, low = rounded.astype(jnp.bfloat16), (sensitivity - rounded).astype(jnp.bfloat16)
        stacked = jnp.concatenate([high, high, low], axis=1)
        fit = pl.pallas_call(
            functools.partial(fit_kernel, dims, sizes),
            out_shape=jax.ShapeDtypeStruct((8, slots), jnp.float32),
            in_specs=[VMEM, SMEM, VMEM],
            out_specs=VMEM,
            scratch_shapes=[pltpu.VMEM((stacked.shape[0], 2 * slots), jnp.float32)],
            name="fit",
        )(ordered, place, stacked)
        force = pl.pallas_call(
            functools.partial(force_kernel, scale),
            out_shape=jax.ShapeDtypeStruct((8, slots), jnp.float32),
            in_specs=[VMEM] * 6 + [SMEM] * 3,
            out_specs=VMEM,
            scratch_shapes=[pltpu.VMEM((slots, 8), jnp.float32)],
            name="pair",
        )(near, near_radius, columns, radius, fit, rank, lists, counts, offsets)[0:3]
        current = current + STEP_SIZE * (living * force)
    shape = positions.shape
    return ((current - start).reshape(shape), force.reshape(shape), evolved)


def solution(mesh):
    placed = (
        P(None, "gx", "gy", "gz", None),
        P("gx", "gy", "gz", None),
        P("gx", "gy", "gz", None),
        P(),
        P("gx", "gy", "gz"),
        P("gx", "gy", "gz"),
    )
    return jax.shard_map(
        on_device,
        mesh=mesh,
        in_specs=placed,
        out_specs=(
            P(None, "gx", "gy", "gz", None),
            P(None, "gx", "gy", "gz", None),
            P("gx", "gy", "gz"),
        ),
        check_vma=False,
    )
```

```python
import functools
import math

import jax
import jax.numpy as jnp
from jax import lax
from jax.experimental import pallas as pl
from jax.experimental.pallas import tpu as pltpu
from jax.sharding import PartitionSpec as P

SPLAT_MARGIN = 3
BLUR_REACH = 2
STEPS = 2
CUTOFF = 10.0
EPSILON = 1e-06
STEP_SIZE = 1.0
FIT_GAIN = 0.2
REACH = SPLAT_MARGIN + BLUR_REACH
PAD = 8
LANES = 128
ROWS = 64
MESH = pl.DeviceIdType.MESH
AXES = ("gx", "gy", "gz")
VMEM = pl.BlockSpec(memory_space=pltpu.VMEM)
SMEM = pl.BlockSpec(memory_space=pltpu.SMEM)


def sides_of(number):
    return (number // 9 - 1, number // 3 % 3 - 1, number % 3 - 1)


def exchange_kernel(sizes, count, everyone, *refs):
    sources = refs[:count]
    position = count
    if everyone:
        part_ref = refs[position]
        position += 1
    outs = refs[position : position + count]
    position += count
    if everyone:
        parts_out = refs[position]
        position += 1
    send, recv = refs[position : position + 2]
    me = tuple(lax.axis_index(axis) for axis in AXES)
    total = sizes[0] * sizes[1] * sizes[2]
    mine = (me[0] * sizes[1] + me[1]) * sizes[2] + me[2]

    def exists(number):
        sides = sides_of(number)
        inside = None
        for axis in range(3):
            place = me[axis] + sides[axis]
            good = (place >= 0) & (place < sizes[axis])
            inside = good if inside is None else inside & good
        return inside

    def target(number):
        sides = sides_of(number)
        return tuple(me[axis] + sides[axis] for axis in range(3))

    def device_at(linear):
        return (
            linear // (sizes[1] * sizes[2]),
            linear // sizes[2] % sizes[1],
            linear % sizes[2],
        )

    others = [number for number in range(27) if number != 13]
    barrier = pltpu.get_barrier_semaphore()
    if everyone:

        def greet(step, carry):
            linear = lax.rem(mine + step, total)
            pl.semaphore_signal(barrier, inc=1, device_id=device_at(linear), device_id_type=MESH)
            return carry

        lax.fori_loop(1, total, greet, 0)
        pl.semaphore_wait(barrier, total - 1)
        send_all, recv_all = refs[position + 2 : position + 4]
    else:
        expected = 1
        for axis in range(3):
            low = jnp.where(me[axis] > 0, 1, 0)
            high = jnp.where(me[axis] < sizes[axis] - 1, 1, 0)
            expected = expected * (1 + low + high)
        for number in others:

            @pl.when(exists(number))
            def _(number=number):
                pl.semaphore_signal(barrier, inc=1, device_id=target(number), device_id_type=MESH)

        pl.semaphore_wait(barrier, expected - 1)

    def outgoing(index, number):
        return pltpu.make_async_remote_copy(
            src_ref=sources[index],
            dst_ref=outs[index].at[26 - number],
            send_sem=send.at[index, number],
            recv_sem=recv.at[index, 26 - number],
            device_id=target(number),
            device_id_type=MESH,
        )

    def arriving(index, number):
        return pltpu.make_async_remote_copy(
            src_ref=sources[index],
            dst_ref=outs[index].at[number],
            send_sem=send.at[index, number],
            recv_sem=recv.at[index, number],
            device_id=target(number),
            device_id_type=MESH,
        )

    def sum_copy(linear, slot):
        return pltpu.make_async_remote_copy(
            src_ref=part_ref,
            dst_ref=parts_out.at[slot],
            send_sem=send_all.at[linear],
            recv_sem=recv_all.at[slot],
            device_id=device_at(linear),
            device_id_type=MESH,
        )

    if everyone:

        def send_sum(step, carry):
            sum_copy(lax.rem(mine + step, total), mine).start()
            return carry

        lax.fori_loop(1, total, send_sum, 0)
    for number in others:

        @pl.when(exists(number))
        def _(number=number):
            for index in range(count):
                outgoing(index, number).start()

    for index in range(count):
        outs[index][13] = sources[index][...]
    if everyone:
        parts_out[mine] = part_ref[...]
    for number in others:

        @pl.when(jnp.logical_not(exists(number)))
        def _(number=number):
            for index in range(count):
                outs[index][number] = jnp.zeros(sources[index].shape, jnp.float32)

    for number in others:

        @pl.when(exists(number))
        def _(number=number):
            for index in range(count):
                outgoing(index, number).wait_send()
                arriving(index, number).wait_recv()

    if everyone:

        def wait_sum(step, carry):
            linear = lax.rem(mine + step, total)
            sum_copy(linear, mine).wait_send()
            sum_copy(linear, linear).wait_recv()
            return carry

        lax.fori_loop(1, total, wait_sum, 0)


def exchange(arrays, part, collective_id):
    sizes = tuple(lax.axis_size(axis) for axis in AXES)
    total = sizes[0] * sizes[1] * sizes[2]
    count = len(arrays)
    everyone = part is not None
    out_shape = [jax.ShapeDtypeStruct((27,) + a.shape, jnp.float32) for a in arrays]
    scratch = [pltpu.SemaphoreType.DMA((count, 27)), pltpu.SemaphoreType.DMA((count, 27))]
    operands = list(arrays)
    if everyone:
        operands.append(part)
        out_shape.append(jax.ShapeDtypeStruct((total,) + part.shape, jnp.float32))
        scratch += [pltpu.SemaphoreType.DMA((total,)), pltpu.SemaphoreType.DMA((total,))]
    return pl.pallas_call(
        functools.partial(exchange_kernel, sizes, count, everyone),
        out_shape=out_shape,
        in_specs=[VMEM] * len(operands),
        out_specs=[VMEM] * len(out_shape),
        scratch_shapes=scratch,
        compiler_params=pltpu.CompilerParams(collective_id=collective_id, has_side_effects=True),
        name=f"exchange{collective_id}",
    )(*operands)


def kernel_weights(reach):
    values = [math.exp(-0.5 * (index - reach) ** 2) for index in range(2 * reach + 1)]
    whole = sum(values)
    return [value / whole for value in values]


def spread(values):
    weights = kernel_weights(BLUR_REACH)
    rows = values.shape[0]
    result = weights[BLUR_REACH] * values
    for shift in range(1, BLUR_REACH + 1):
        both = pltpu.roll(values, shift, 0) + pltpu.roll(values, rows - shift, 0)
        result = result + weights[BLUR_REACH + shift] * both
    return result


def profile_rows(coord, side, length, place, extent, slope):
    rows = length + 2 * PAD
    point = lax.broadcasted_iota(jnp.int32, (rows, coord.shape[-1]), 0) - PAD
    within = point + place * length
    start = side * length
    grid = (within >= 0) & (within < extent * length)
    window = grid & (point >= start - SPLAT_MARGIN) & (point < start + length + SPLAT_MARGIN)
    reach = grid & (point >= start - REACH) & (point < start + length + REACH)
    offset = jnp.asarray(side * length, jnp.float32)
    gap = point.astype(jnp.float32) - (coord + offset)
    plain = jnp.where(window, jnp.exp(-0.5 * gap * gap), 0.0)
    wide = jnp.where(reach, spread(plain), 0.0)
    if not slope:
        return wide
    return wide, jnp.where(reach, spread(gap * plain), 0.0)


def move(values, onehot):
    rows = values.shape[0]
    first = values.astype(jnp.bfloat16).astype(jnp.float32)
    rest = values - first
    second = rest.astype(jnp.bfloat16).astype(jnp.float32)
    stacked = jnp.concatenate([first, second, rest - second], axis=0).astype(jnp.bfloat16)
    moved = jnp.dot(stacked, onehot.astype(jnp.bfloat16), preferred_element_type=jnp.float32)
    return moved[0:rows] + (moved[rows : 2 * rows] + moved[2 * rows : 3 * rows])


def sort_kernel(own_ref, chunk_ref, column_ref, row_ref, rank_ref):
    slots = own_ref.shape[-1]
    own = own_ref[...]
    turned = own.T
    first = lax.broadcasted_iota(jnp.int32, (slots, slots), 0)
    second = lax.broadcasted_iota(jnp.int32, (slots, slots), 1)
    earlier = second < first
    far = 9.0e3
    part_row = jnp.zeros((1, slots), jnp.float32)
    part_column = jnp.zeros((slots, 1), jnp.float32)
    for axis, size in ((0, slots // 2), (1, LANES), (2, 1)):
        row = jnp.where(own[7:8, :] > 0.5, jnp.clip(own[axis : axis + 1, :], -5.0e3, 5.0e3), far)
        column = jnp.where(
            turned[:, 7:8] > 0.5, jnp.clip(turned[:, axis : axis + 1], -5.0e3, 5.0e3), far
        )
        row = row + 1.0e5 * part_row
        column = column + 1.0e5 * part_column
        before = jnp.where((row < column) | ((row == column) & earlier), 1.0, 0.0)
        rank_column = jnp.sum(before, axis=1, keepdims=True)
        rank_row = float(slots - 1) - jnp.sum(before, axis=0, keepdims=True)
        part_column = jnp.floor(rank_column * (1.0 / size))
        part_row = jnp.floor(rank_row * (1.0 / size))
    place = jnp.where(rank_column.astype(jnp.int32) == second, 1.0, 0.0)
    ordered = move(own, place)
    row_ref[...] = ordered
    column_ref[...] = ordered.T
    for k in range(slots // LANES):
        chunk_ref[k] = ordered[:, k * LANES : (k + 1) * LANES]
    rank_ref[...] = rank_row.astype(jnp.int32)


def born_kernel(
    near_ref, own_ref, list_ref, count_ref, offset_ref, out_ref, row_ref, held_ref
):
    slots = own_ref.shape[0]
    held_ref[...] = jnp.zeros_like(held_ref)

    def block(index, carry):
        base = pl.multiple_of(index * ROWS, ROWS)
        own = [
            jnp.broadcast_to(own_ref[pl.ds(base, ROWS), k : k + 1], (ROWS, LANES))
            for k in range(3)
        ]

        many = count_ref[0, index]

        def visit(step, summed):
            following = 2 * step + 1
            more = following < many
            number = jnp.where(more, list_ref[index, following], 13 * (slots // LANES))
            summed = meet(list_ref[index, 2 * step], 1.0, summed)
            return meet(number, jnp.where(more, 1.0, 0.0), summed)

        def meet(number, factor, summed):
            squared = None
            for axis in range(3):
                row = near_ref[number, axis : axis + 1, :] + offset_ref[number, axis]
                gap = own[axis] - row
                squared = gap * gap if squared is None else squared + gap * gap
            smooth = jnp.maximum(1.0 - squared * (1.0 / (CUTOFF * CUTOFF)), 0.0)
            weight = near_ref[number, 4:5, :] * factor
            return summed + jnp.exp(squared * -0.125) * (smooth * smooth) * weight

        summed = lax.fori_loop(
            0, (many + 1) // 2, visit, jnp.zeros((ROWS, LANES), jnp.float32)
        )
        own_screen = own_ref[pl.ds(base, ROWS), 4:5]
        radius = own_ref[pl.ds(base, ROWS), 6:7]
        found = radius + (jnp.sum(summed, axis=1, keepdims=True) - own_screen)
        out_ref[pl.ds(base, ROWS), :] = found
        held_ref[pl.ds(base, ROWS), 0:1] = found
        return carry

    lax.fori_loop(0, slots // ROWS, block, 0)
    turned = held_ref[...].T
    for piece in range(slots // LANES):
        row_ref[piece] = turned[0:1, piece * LANES : (piece + 1) * LANES]


def force_kernel(
    scale, near_ref, radii_ref, own_ref, radius_ref, fit_ref, rank_ref, list_ref, count_ref,
    offset_ref, out_ref, held_ref,
):
    slots = own_ref.shape[0]
    held_ref[...] = jnp.zeros_like(held_ref)

    def block(index, carry):
        base = pl.multiple_of(index * ROWS, ROWS)
        own = [
            jnp.broadcast_to(own_ref[pl.ds(base, ROWS), k : k + 1], (ROWS, LANES))
            for k in range(3)
        ]
        radius = jnp.broadcast_to(radius_ref[pl.ds(base, ROWS), :], (ROWS, LANES))
        inverse_radius = -0.25 / radius

        many = count_ref[0, index]

        def visit(step, summed):
            following = 2 * step + 1
            more = following < many
            number = jnp.where(more, list_ref[index, following], 13 * (slots // LANES))
            summed = meet(list_ref[index, 2 * step], 1.0, summed)
            return meet(number, jnp.where(more, 1.0, 0.0), summed)

        def meet(number, factor, summed):
            squared = None
            gaps = []
            for axis in range(3):
                row = near_ref[number, axis : axis + 1, :] + offset_ref[number, axis]
                gap = own[axis] - row
                gaps.append(gap)
                squared = gap * gap if squared is None else squared + gap * gap
            smooth = jnp.maximum(1.0 - squared * (1.0 / (CUTOFF * CUTOFF)), 0.0)
            near_radius = radii_ref[number]
            charge = near_ref[number, 3:4, :] * factor
            fading = jnp.exp(squared * (inverse_radius * (1.0 / near_radius)))
            inverse = lax.rsqrt(squared + (radius * near_radius) * fading)
            common = (charge * (smooth * inverse)) * (
                2.0 / (CUTOFF * CUTOFF)
                + (smooth * (inverse * inverse)) * (0.5 - 0.125 * fading)
            )
            return tuple(total + common * gap for total, gap in zip(summed, gaps))

        zero = jnp.zeros((ROWS, LANES), jnp.float32)
        summed = lax.fori_loop(0, (many + 1) // 2, visit, (zero, zero, zero))
        charge = own_ref[pl.ds(base, ROWS), 3:4]
        for axis in range(3):
            held_ref[pl.ds(base, ROWS), axis : axis + 1] = -charge * jnp.sum(
                summed[axis], axis=1, keepdims=True
            )
        return carry

    lax.fori_loop(0, slots // ROWS, block, 0)
    force = held_ref[...].T + scale * fit_ref[...]
    slot = lax.broadcasted_iota(jnp.int32, (slots, slots), 0)
    back = jnp.where(slot == rank_ref[...], 1.0, 0.0)
    out_ref[...] = move(force, back)


def halves(value):
    high = value.astype(jnp.bfloat16)
    return high, (value - high.astype(jnp.float32)).astype(jnp.bfloat16)


def evolved_kernel(
    dims, sizes, near_ref, map_ref, place_ref, out_ref, part_ref, px_ref, py_ref, pz_ref, total_ref
):
    places = [place_ref[0, k] for k in range(3)]
    pieces = near_ref.shape[0] // 27
    depth = dims[2]

    def there(sides):
        inside = None
        for axis in range(3):
            spot = places[axis] + sides[axis]
            good = (spot >= 0) & (spot < sizes[axis])
            inside = good if inside is None else inside & good
        return inside

    def profiles(cell, carry):
        sides = sides_of(cell)

        @pl.when(there(sides))
        def _():
            for piece in range(pieces):
                atoms = near_ref.at[cell * pieces + piece]
                lanes = slice(piece * LANES, (piece + 1) * LANES)
                made = [
                    profile_rows(
                        atoms[axis : axis + 1, :],
                        sides[axis],
                        dims[axis],
                        places[axis],
                        sizes[axis],
                        False,
                    )[PAD : PAD + dims[axis]]
                    for axis in range(3)
                ]
                px_ref[cell, :, lanes] = made[0] * atoms[5:6, :]
                py_ref[cell, :, lanes] = made[1]
                high, low = halves(made[2])
                pz_ref[cell, 0:depth, lanes] = high
                pz_ref[cell, depth : 2 * depth, lanes] = low

        return carry

    lax.fori_loop(0, 27, profiles, 0)
    out_ref[...] = jnp.zeros_like(out_ref)
    spans_x = ((0, REACH), (0, dims[0]), (dims[0] - REACH, dims[0]))
    spans_y = ((0, PAD), (0, dims[1]), (dims[1] - PAD, dims[1]))
    for ix in range(3):
        for iy in range(3):
            x0, x1 = spans_x[ix]
            y0, y1 = spans_y[iy]
            rows = (x1 - x0) * (y1 - y0)

            @pl.when(there((ix - 1, iy - 1, 0)))
            def _(ix=ix, iy=iy, x0=x0, x1=x1, y0=y0, y1=y1, rows=rows):
                total_ref[0 : 2 * rows, :] = jnp.zeros((2 * rows, 2 * depth), jnp.float32)

                def add(iz, carry):
                    cell = ix * 9 + iy * 3 + iz

                    @pl.when(there((ix - 1, iy - 1, iz - 1)))
                    def _():
                        py = py_ref[cell, y0:y1, :]
                        pieces_high, pieces_low = [], []
                        for k in range(x0, x1):
                            value = px_ref[cell, k : k + 1, :] * py
                            upper = value.astype(jnp.bfloat16).astype(jnp.float32)
                            pieces_high.append(upper)
                            pieces_low.append(value - upper)
                        plane = jnp.concatenate(pieces_high + pieces_low, axis=0)
                        total_ref[0 : 2 * rows, :] += lax.dot_general(
                            plane.astype(jnp.bfloat16),
                            pz_ref[cell],
                            (((1,), (1,)), ((), ())),
                            preferred_element_type=jnp.float32,
                        )

                    return carry

                lax.fori_loop(0, 3, add, 0)
                result = (
                    total_ref[0:rows, 0:depth]
                    + total_ref[0:rows, depth : 2 * depth]
                    + total_ref[rows : 2 * rows, 0:depth]
                )
                out_ref[x0:x1, y0:y1, :] += result.reshape(x1 - x0, y1 - y0, depth)

    evolved = out_ref[...]
    given = map_ref[...]
    lane = lax.broadcasted_iota(jnp.int32, (1, LANES), 1)
    part_ref[...] = jnp.where(
        lane == 0,
        jnp.sum(evolved * evolved),
        jnp.where(
            lane == 1,
            jnp.sum(evolved * given),
            jnp.where(lane == 2, jnp.sum(given * given), 0.0),
        ),
    )


def fit_kernel(dims, sizes, own_ref, place_ref, sens_ref, out_ref, big_ref):
    places = [place_ref[0, k] for k in range(3)]
    slots = own_ref.shape[-1]
    wide = []
    slope = []
    for axis in range(3):
        a, b = profile_rows(
            own_ref[axis : axis + 1, :], 0, dims[axis], places[axis], sizes[axis], True
        )
        wide.append(a)
        slope.append(b)
    both = jnp.concatenate([wide[2], slope[2]], axis=1)
    high, low = halves(both)
    right = jnp.concatenate([high, low, high], axis=0)
    big_ref[...] = jnp.dot(sens_ref[...], right, preferred_element_type=jnp.float32)
    height = dims[1] + 2 * PAD
    force = [jnp.zeros((1, slots), jnp.float32) for _ in range(3)]
    for k in range(dims[0] + 2 * REACH):
        row = PAD - REACH + k
        plain_z = big_ref[k * height : (k + 1) * height, 0:slots]
        slope_z = big_ref[k * height : (k + 1) * height, slots : 2 * slots]
        plain = jnp.sum(plain_z * wide[1], axis=0, keepdims=True)
        turned_y = jnp.sum(plain_z * slope[1], axis=0, keepdims=True)
        turned_z = jnp.sum(slope_z * wide[1], axis=0, keepdims=True)
        here = wide[0][row : row + 1, :]
        force[0] = force[0] + slope[0][row : row + 1, :] * plain
        force[1] = force[1] + here * turned_y
        force[2] = force[2] + here * turned_z
    mass = own_ref[5:6, :]
    out_ref[...] = jnp.zeros_like(out_ref)
    for axis in range(3):
        out_ref[axis : axis + 1, :] = mass * force[axis]


def frame_kernel(dims, cube_ref, out_ref):
    reaches = (REACH, PAD, PAD)

    def span(side, axis):
        length, reach = dims[axis], reaches[axis]
        if side == 0:
            return slice(length - reach, length), slice(0, reach)
        if side == 1:
            return slice(0, length), slice(reach, reach + length)
        return slice(0, reach), slice(reach + length, length + 2 * reach)

    for a in range(3):
        from_x, to_x = span(a, 0)
        for b in range(3):
            from_y, to_y = span(b, 1)
            out_ref[to_x, to_y, :] = jnp.concatenate(
                [
                    cube_ref[a * 9 + b * 3 + c, from_x, from_y, :][:, :, span(c, 2)[0]]
                    for c in range(3)
                ],
                axis=2,
            )


def frame_map(bricks, dims):
    return pl.pallas_call(
        functools.partial(frame_kernel, dims),
        out_shape=jax.ShapeDtypeStruct(
            (dims[0] + 2 * REACH, dims[1] + 2 * PAD, dims[2] + 2 * PAD), jnp.float32
        ),
        in_specs=[VMEM],
        out_specs=VMEM,
        name="frame",
    )(bricks.reshape((27,) + dims))


def active_lists(near, columns, offsets):
    whole = near.shape[0]
    slots = columns.shape[0]
    blocks = slots // ROWS
    coords = near[:, 0:3, :] + offsets[:, :, None]
    live = near[:, 7:8, :] > 0.5
    big = 1e30
    low = jnp.where(live, coords, big).min(axis=-1)
    high = jnp.where(live, coords, -big).max(axis=-1)
    grouped = columns.reshape(blocks, ROWS, columns.shape[1])
    own_live = grouped[:, :, 7:8] > 0.5
    own_low = jnp.where(own_live, grouped[:, :, 0:3], big).min(axis=1)
    own_high = jnp.where(own_live, grouped[:, :, 0:3], -big).max(axis=1)
    apart = jnp.maximum(
        low[None, :, :] - own_high[:, None, :], own_low[:, None, :] - high[None, :, :]
    )
    apart = jnp.maximum(apart, 0.0)
    keep = jnp.sum(apart * apart, axis=-1) < CUTOFF * CUTOFF * 1.001
    index = jnp.arange(whole, dtype=jnp.int32)
    before = (index[:, None] <= index[None, :]).astype(jnp.bfloat16)
    spot = jnp.dot(
        keep.astype(jnp.bfloat16), before, preferred_element_type=jnp.float32
    ).astype(jnp.int32)
    counts = spot[:, -1]
    chosen = keep[:, :, None] & (spot[:, :, None] - 1 == index[None, None, :])
    lists = jnp.sum(jnp.where(chosen, index[None, :, None], 0), axis=1)
    return lists, counts[None, :]


def on_device(positions, charges, atom_types, type_table, live_count, exp_map):
    dims = exp_map.shape
    sizes = tuple(lax.axis_size(axis) for axis in AXES)
    slots = positions.shape[-1]
    grid_points = dims[0] * dims[1] * dims[2] * sizes[0] * sizes[1] * sizes[2]
    scale = FIT_GAIN * float(grid_points)
    place = jnp.stack([lax.axis_index(axis) for axis in AXES]).astype(jnp.int32).reshape(1, 3)

    kinds = jnp.arange(type_table.shape[1], dtype=jnp.int32)
    onehot = (atom_types.reshape(1, slots) == kinds[:, None]).astype(jnp.float32)
    props = jnp.sum(type_table[:, :, None] * onehot[None], axis=1)
    living = (
        lax.broadcasted_iota(jnp.int32, (1, slots), 1) < live_count.reshape(1, 1)
    ).astype(jnp.float32)
    start = positions.reshape(3, slots)
    fixed = jnp.concatenate(
        [
            charges.reshape(1, slots) * living,
            props[1:2] * living,
            props[2:3] * living,
            props[0:1],
            living,
        ],
        axis=0,
    )
    current = start
    pieces = slots // LANES
    number = jnp.arange(27 * pieces, dtype=jnp.int32) // pieces
    offsets = jnp.stack(sides_of(number), axis=1).astype(jnp.float32) * jnp.array(
        dims, jnp.float32
    )
    framed = None
    for step in range(STEPS):
        own = jnp.concatenate([current, fixed], axis=0)
        chunks, columns, ordered, rank = pl.pallas_call(
            sort_kernel,
            out_shape=[
                jax.ShapeDtypeStruct((pieces, 8, LANES), jnp.float32),
                jax.ShapeDtypeStruct((slots, 8), jnp.float32),
                jax.ShapeDtypeStruct((8, slots), jnp.float32),
                jax.ShapeDtypeStruct((1, slots), jnp.int32),
            ],
            in_specs=[VMEM],
            out_specs=[VMEM] * 4,
            name="sort",
        )(own)
        if step == 0:
            near, bricks = exchange([chunks, exp_map.reshape(-1, LANES)], None, 0)
            framed = frame_map(bricks, dims)
        else:
            (near,) = exchange([chunks], None, 1)
        near = near.reshape(27 * pieces, 8, LANES)
        lists, counts = active_lists(near, columns, offsets)
        radius, radius_rows = pl.pallas_call(
            born_kernel,
            out_shape=[
                jax.ShapeDtypeStruct((slots, 1), jnp.float32),
                jax.ShapeDtypeStruct((pieces, 1, LANES), jnp.float32),
            ],
            in_specs=[VMEM, VMEM, SMEM, SMEM, SMEM],
            out_specs=[VMEM, VMEM],
            scratch_shapes=[pltpu.VMEM((slots, 8), jnp.float32)],
            name="born",
        )(near, columns, lists, counts, offsets)
        evolved, part = pl.pallas_call(
            functools.partial(evolved_kernel, dims, sizes),
            out_shape=[
                jax.ShapeDtypeStruct(dims, jnp.float32),
                jax.ShapeDtypeStruct((1, LANES), jnp.float32),
            ],
            in_specs=[VMEM, VMEM, SMEM],
            out_specs=[VMEM, VMEM],
            scratch_shapes=[
                pltpu.VMEM((27, dims[0], slots), jnp.float32),
                pltpu.VMEM((27, dims[1], slots), jnp.float32),
                pltpu.VMEM((27, 2 * dims[2], slots), jnp.bfloat16),
                pltpu.VMEM((2 * dims[0] * dims[1], 2 * dims[2]), jnp.float32),
            ],
            name="evolve",
        )(near, exp_map, place)
        near_radius, halo, parts = exchange(
            [radius_rows, evolved.reshape(-1, LANES)], part, 2
        )
        near_radius = near_radius.reshape(27 * pieces, 1, LANES)
        wide = frame_map(halo, dims)
        sums = jnp.sum(parts, axis=(0, 1))
        squares, cross_sum, whole_target = sums[0], sums[1], sums[2]
        norm = jnp.sqrt((squares + EPSILON) * (whole_target + EPSILON))
        score = cross_sum / norm
        sensitivity = framed / norm - score * wide / (squares + EPSILON)
        sensitivity = sensitivity.reshape(-1, sensitivity.shape[-1])
        rounded = lax.reduce_precision(sensitivity, 8, 7)
        high, low = rounded.astype(jnp.bfloat16), (sensitivity - rounded).astype(jnp.bfloat16)
        stacked = jnp.concatenate([high, high, low], axis=1)
        fit = pl.pallas_call(
            functools.partial(fit_kernel, dims, sizes),
            out_shape=jax.ShapeDtypeStruct((8, slots), jnp.float32),
            in_specs=[VMEM, SMEM, VMEM],
            out_specs=VMEM,
            scratch_shapes=[pltpu.VMEM((stacked.shape[0], 2 * slots), jnp.float32)],
            name="fit",
        )(ordered, place, stacked)
        force = pl.pallas_call(
            functools.partial(force_kernel, scale),
            out_shape=jax.ShapeDtypeStruct((8, slots), jnp.float32),
            in_specs=[VMEM] * 6 + [SMEM] * 3,
            out_specs=VMEM,
            scratch_shapes=[pltpu.VMEM((slots, 8), jnp.float32)],
            name="pair",
        )(near, near_radius, columns, radius, fit, rank, lists, counts, offsets)[0:3]
        current = current + STEP_SIZE * (living * force)
    shape = positions.shape
    return ((current - start).reshape(shape), force.reshape(shape), evolved)


def solution(mesh):
    placed = (
        P(None, "gx", "gy", "gz", None),
        P("gx", "gy", "gz", None),
        P("gx", "gy", "gz", None),
        P(),
        P("gx", "gy", "gz"),
        P("gx", "gy", "gz"),
    )
    return jax.shard_map(
        on_device,
        mesh=mesh,
        in_specs=placed,
        out_specs=(
            P(None, "gx", "gy", "gz", None),
            P(None, "gx", "gy", "gz", None),
            P("gx", "gy", "gz"),
        ),
        check_vma=False,
    )
```
